512 devices in a mesh: lat: 16 (over z_hi, y), lon: 32 (over z_lo, x, core).
Axes of the slice: x: 4, y: 4, z: 16 (z_hi: 4, z_lo: 4; z = z_hi * 4 + z_lo), core: 2. Of those that a mesh axis runs over, the one named last changes fastest.
Arguments:
- queries: float32 [64, 1024, 512], P('lat', 'lon'), may hold values from -80 to 80
- key_rows: float32 [512, 512], P(('lat', 'lon')), may hold values from -8 to 8
- value_rows: float32 [512, 512], P(('lat', 'lon')), may hold values from -6 to 6
- cotangent: float32 [64, 1024, 512], P('lat', 'lon'), may hold values from -25 to 25
- conv_taps: float32 [9, 512], replicated, may hold values from -1.75 to 1.75
Outputs:
- query_grad: float32 [64, 1024, 512], P('lat', 'lon')
- key_grad: float32 [512, 512], P(('lat', 'lon'))
- value_grad: float32 [512, 512], P(('lat', 'lon'))
- tap_update: float32 [9, 512], replicated
The draws below stay inside these ranges and needn't reach their ends.
All inputs are finite; a program needn't handle non-finite values.
Results may differ from the reference program's by a relative error of at most 0.0003.
Values sent between devices are 32-bit elements; how exact they have to be, the bound alone decides.
A program may use at most 64 MiB of HBM per device.

```python
import math
import jax
import jax.numpy as jnp
from jax import lax

HD = 64
CH = 512
NLAT = 64
NLON = 1024
KEYS = 512


def attention_inputs(key):
    base_key = jax.random.fold_in(key, 7)
    key_keys, key_queries = jax.random.split(base_key, 2)
    key_table = 2.0 * jnp.clip(jax.random.normal(key_keys, (KEYS, CH), jnp.float32), -4.0, 4.0)
    query_table = jnp.clip(jax.random.normal(key_queries, (NLAT * NLON, CH), jnp.float32), -4.0, 4.0)
    return (query_table.reshape(NLAT, NLON, CH), key_table)


def draw_queries(key, part):
    return attention_inputs(key)[0]


def draw_key_rows(key, part):
    return attention_inputs(key)[1]


def draw_cotangent(key, part):
    key_scale, key_noise = jax.random.split(jax.random.fold_in(key, 11), 2)
    channel_scale = jnp.exp(jax.random.uniform(key_scale, (CH,), jnp.float32, math.log(0.3), math.log(3.0)))
    return jnp.clip(jax.random.normal(key_noise, (NLAT, NLON, CH), jnp.float32), -4.0, 4.0) * channel_scale


def levels(stream_key, extent, shards, low, largest):
    factor_of = 1.0
    for dim, parts in shards:
        draws = jax.random.uniform(jax.random.fold_in(jax.random.fold_in(stream_key, 6), dim), (parts,), jnp.float32, low / len(shards), largest / len(shards))
        factor_of = factor_of * jnp.repeat(jnp.exp(draws), extent[dim] // parts).reshape((-1,) + (1,) * (len(extent) - 1 - dim))
    return factor_of


def normal_values(stream_key, dims, spread, most, pieces=(), held_as=jnp.bfloat16):
    result = spread * jax.random.normal(stream_key, dims, jnp.float32)
    if pieces:
        result = result * levels(stream_key, dims, pieces, -0.22, 0.18)
    return jnp.clip(result, -most, most).astype(held_as)


def setup_inputs(seed: int = 0) -> dict:
    key_list = jax.random.split(jax.random.key(seed), 6)
    queries = draw_queries(jax.random.fold_in(key_list[5], 71), 0)
    key_rows = draw_key_rows(jax.random.fold_in(key_list[5], 71), 0)
    value_rows = normal_values(key_list[2], (KEYS, CH), 1.0, 6.0, ((0, 512),), jnp.float32)
    cotangent = draw_cotangent(jax.random.fold_in(key_list[5], 71), 0)
    conv_taps = normal_values(key_list[4], (9, CH), 0.35, 1.75, (), jnp.float32)
    return dict(queries=queries, key_rows=key_rows, value_rows=value_rows, cotangent=cotangent, conv_taps=conv_taps)


HIGH = lax.Precision.HIGHEST
OFFSETS = ((-1, -1), (-1, 0), (-1, 1), (0, -1), (0, 0), (0, 1), (1, -1), (1, 0), (1, 1))

def split_heads(matrix):
    return matrix.reshape(matrix.shape[0], -1, HD)

def soft_scores(query_part, key_part):
    logits = jnp.einsum('qhd,khd->hqk', split_heads(query_part), split_heads(key_part), precision=HIGH) * HD ** (-0.5)
    row_peak = lax.optimization_barrier(jnp.max(logits, -1, keepdims=True))
    raised = jnp.exp(logits - row_peak)
    return raised / lax.optimization_barrier(jnp.sum(raised, -1, keepdims=True))

def latitude_weights():
    centres = (jnp.arange(NLAT, dtype=jnp.float32) + 0.5) * (jnp.pi / NLAT)
    cosine = jnp.sin(centres)
    return cosine / (jnp.sum(cosine) / NLAT)

def pad_field(grid_field):
    wrapped = jnp.pad(grid_field, ((0, 0), (1, 1), (0, 0)), mode='wrap')
    return jnp.pad(wrapped, ((1, 1), (0, 0), (0, 0)))

def reference(queries, key_rows, value_rows, cotangent, conv_taps):
    value_heads = split_heads(value_rows)
    key_heads = split_heads(key_rows)

    def forward_row(query_row):
        soft_weights = soft_scores(query_row, key_rows)
        return jnp.einsum('hqk,khd->qhd', soft_weights, value_heads, precision=HIGH).reshape(query_row.shape)
    attn_out = lax.map(forward_row, queries)
    weighted = cotangent * latitude_weights()[:, None, None]
    grad_padded = pad_field(weighted)
    out_padded = pad_field(attn_out)
    out_grad = weighted
    tap_list = []
    for tap_index, (shift_row, shift_col) in enumerate(OFFSETS):
        out_grad = out_grad + conv_taps[tap_index] * grad_padded[1 - shift_row:1 - shift_row + NLAT, 1 - shift_col:1 - shift_col + NLON]
        tap_list.append(lax.optimization_barrier(jnp.sum(out_padded[1 + shift_row:1 + shift_row + NLAT, 1 + shift_col:1 + shift_col + NLON] * weighted, axis=(0, 1))))
    tap_sum = jnp.stack(tap_list)
    tap_update = tap_sum / jnp.sqrt(jnp.mean(tap_sum * tap_sum) + 1e-06)

    def backward_row(running, inputs):
        key_acc, value_acc = running
        query_row, grad_row, out_row = inputs
        soft_weights = soft_scores(query_row, key_rows)
        grad_heads = split_heads(grad_row)
        value_acc = value_acc + jnp.einsum('hqk,qhd->khd', soft_weights, grad_heads, precision=HIGH).reshape(key_rows.shape)
        prob_grad = jnp.einsum('qhd,khd->hqk', grad_heads, value_heads, precision=HIGH)
        row_dot = jnp.transpose(lax.optimization_barrier(jnp.sum(grad_heads * split_heads(out_row), -1)))[:, :, None]
        logit_grad = soft_weights * (prob_grad - row_dot)
        query_part = (jnp.einsum('hqk,khd->qhd', logit_grad, key_heads, precision=HIGH) * HD ** (-0.5)).reshape(query_row.shape)
        key_acc = key_acc + (jnp.einsum('hqk,qhd->khd', logit_grad, split_heads(query_row), precision=HIGH) * HD ** (-0.5)).reshape(key_rows.shape)
        return ((key_acc, value_acc), query_part)
    zeros_acc = jnp.zeros(key_rows.shape, jnp.float32)
    (key_grad, value_grad), query_grad = lax.scan(backward_row, (zeros_acc, zeros_acc), (queries, out_grad, attn_out))
    return (query_grad, key_grad, value_grad, tap_update)
```

```python
import functools

import jax
import jax.numpy as jnp
import numpy as np
from jax import lax
from jax.experimental import pallas as pl
from jax.experimental.pallas import tpu as pltpu
from jax.sharding import PartitionSpec as P

HD = 64
NX = 4
NY = 4
ROWS = 4
COLS = 32
F32 = jnp.float32
BF16 = jnp.bfloat16
MESH = pl.DeviceIdType.MESH


def low_lanes(shape):
    return lax.broadcasted_iota(jnp.int32, shape, len(shape) - 1) < HD


def swap(value):
    return pltpu.roll(value, HD, value.ndim - 1)


def both_low(first, second):
    return jnp.where(low_lanes(first.shape), first, swap(second))


def both_high(first, second):
    return jnp.where(low_lanes(first.shape), swap(first), second)


def split2(value):
    high = value.astype(BF16)
    return high, (value - high.astype(F32)).astype(BF16)


def split3(value):
    first = value.astype(BF16)
    rest = value - first.astype(F32)
    second = rest.astype(BF16)
    return first, second, (rest - second.astype(F32)).astype(BF16)


def dot(a, b):
    return jnp.dot(a, b, preferred_element_type=F32)


def kernel(
    sizes,
    q_ref, c_ref, k_ref, v_ref, t_ref,
    dq_ref, dk_ref, dv_ref, tu_ref,
    ws, qs, wx, qx, kvs, kvx, kvy, hus, hds, hu, hd, hb,
    taps, bs, bd, rq, ro, ak, av, kt, vt, ph, plo, dh, dlo, op, dqs, dqr,
    dkvb, rsy, zs, rsz, fxs, fxr, txs, txr,
    w_s, w_r, q_s, q_r, kx_s, kx_r, z_s, z_r, y_s, y_r, h_s, h_r,
    d_s, d_r, ry_s, ry_r, rz_s, rz_r, fx_s, fx_r, tx_s, tx_r,
):
    nx, ny, nzl, nzh = sizes
    group = 2 * nx
    nz = nzl * nzh
    band_count = nzh * ny
    wide = group * COLS
    keys = ny * nz * group
    channels = group * HD
    lat = lax.axis_index("lat")
    lon = lax.axis_index("lon")
    y = lax.rem(lat, ny)
    z_hi = lax.div(lat, ny)
    z_lo = lax.div(lon, group)
    g = lax.rem(lon, group)
    z = z_hi * nzl + z_lo

    def at(z_of, y_of, g_of):
        return (lax.div(z_of, nzl) * ny + y_of, lax.rem(z_of, nzl) * group + g_of)

    def around(value, step, count):
        return lax.rem(value + step + count, count)

    x_peers = [at(z, y, around(g, e, group)) for e in range(1, group)]
    z_peers = [at(around(z, e, nz), y, g) for e in range(1, nz)]
    y_peers = [at(z, around(y, e, ny), g) for e in range(1, ny)]

    def beside(d_lat, d_lon):
        return (around(lat, d_lat, band_count), around(z_lo, d_lon, nzl) * group + g)

    h_steps = [(1, 0), (-1, 0)] + [(a, b) for a in (-1, 0, 1) for b in (1, -1)]
    h_peers = [beside(a, b) for a, b in h_steps]

    barrier = pltpu.get_barrier_semaphore()
    partners = x_peers + z_peers + y_peers + h_peers
    for peer in partners:
        pl.semaphore_signal(barrier, inc=1, device_id=peer, device_id_type=MESH)

    def send(source, target, send_sem, recv_sem, peer):
        copy = pltpu.make_async_remote_copy(
            src_ref=source, dst_ref=target, send_sem=send_sem, recv_sem=recv_sem,
            device_id=peer, device_id_type=MESH,
        )
        copy.start()
        return copy

    started = []

    for m in range(group // 2):
        cut = slice(m * 128, (m + 1) * 128)
        k_part = k_ref[:, cut]
        v_part = v_ref[:, cut]
        kvs[2 * m] = both_low(k_part, v_part)
        kvs[2 * m + 1] = both_high(k_part, v_part)
    line_total = ROWS * band_count
    centres = (np.arange(line_total) + 0.5) * np.pi / line_total
    mean_cosine = float(np.mean(np.sin(centres)))
    line = lax.broadcasted_iota(jnp.int32, (8, 128), 0) + lat * ROWS
    weight = jnp.sin((line.astype(F32) + 0.5) * (np.pi / line_total)) / mean_cosine
    for m in range(group // 2):
        cut = slice(m * 128, (m + 1) * 128)
        for r in range(2):
            upper = c_ref[r, :, cut] * weight[r : r + 1]
            lower = c_ref[r + 2, :, cut] * weight[r + 2 : r + 3]
            ws[2 * m, r] = both_low(upper, lower)
            ws[2 * m + 1, r] = both_high(upper, lower)
    for m in range(group // 2):
        cut = slice(m * 128, (m + 1) * 128)
        for r in range(2):
            upper = q_ref[r, :, cut] * (HD ** -0.5)
            lower = q_ref[r + 2, :, cut] * (HD ** -0.5)
            qs[2 * m, r] = both_low(upper, lower)
            qs[2 * m + 1, r] = both_high(upper, lower)
    own_w = pl.multiple_of(8 + COLS * g, 8)
    own_q = pl.multiple_of(COLS * g, 8)

    pl.semaphore_wait(barrier, len(partners))

    kx_copies = []
    for e, peer in enumerate(x_peers):
        to = around(g, e + 1, group)
        kx_copies.append(send(kvs.at[to], kvx.at[g], kx_s.at[e], kx_r.at[e], peer))
    w_copies = []
    for e, peer in enumerate(x_peers):
        to = around(g, e + 1, group)
        target = wx.at[pl.ds(1, 2), pl.ds(own_w, COLS), :]
        w_copies.append(send(ws.at[to], target, w_s.at[e], w_r.at[e], peer))
    q_copies = []
    for e, peer in enumerate(x_peers):
        to = around(g, e + 1, group)
        target = qx.at[:, pl.ds(own_q, COLS), :]
        q_copies.append(send(qs.at[to], target, q_s.at[e], q_r.at[e], peer))
    kvx[g] = kvs[g]
    wx[pl.ds(1, 2), pl.ds(own_w, COLS), :] = ws[g]
    qx[:, pl.ds(own_q, COLS), :] = qs[g]

    for copy in kx_copies:
        copy.wait_recv()
    kvy[y, z] = jnp.concatenate([kvx[j] for j in range(group)], 0)
    z_copies = []
    for e, peer in enumerate(z_peers):
        z_copies.append(send(kvy.at[y, z], kvy.at[y, z], z_s.at[e], z_r.at[e], peer))

    for copy in w_copies:
        copy.wait_recv()
    half = wide // 2
    hus[...] = both_high(wx[2, 8 : 8 + half], wx[2, 8 + half : 8 + wide])
    hds[...] = both_low(wx[1, 8 : 8 + half], wx[1, 8 + half : 8 + wide])
    h_copies = []
    for i, (a, b) in enumerate(h_steps):
        if b == 0:
            source, target = (hus, hu) if a == 1 else (hds, hd)
        else:
            source = wx.at[pl.ds(1, 2), pl.ds(wide if b == 1 else 8, 8), :]
            target = hb.at[i - 2]
        h_copies.append(send(source, target, h_s.at[i], h_r.at[i], h_peers[i]))

    for copy in q_copies:
        copy.wait_recv()
    for r in range(2):
        value = qx[r]
        high = value.astype(BF16).astype(F32)
        low = value - high
        rq[r] = both_low(high, low).astype(BF16)
        rq[r + 2] = both_high(high, low).astype(BF16)
        q1, q2, q3 = split3(jnp.transpose(value))
        for part in range(2):
            rows = slice(part * HD, (part + 1) * HD)
            for place, piece in enumerate((q1, q2, q1, q2, q3, q1)):
                bs[r + 2 * part, place * HD : (place + 1) * HD] = piece[rows]

    for copy in z_copies:
        copy.wait_recv()
    y_copies = []
    for e, peer in enumerate(y_peers):
        y_copies.append(send(kvy.at[y], kvy.at[y], y_s.at[e], y_r.at[e], peer))

    pair = pl.multiple_of(lax.div(g, 2) * 128, 128)
    taps[0:9] = t_ref[:, pl.ds(pair, 128)]
    taken = taps[...]
    low = low_lanes(taken.shape)
    even = jnp.where(low, taken, swap(taken))
    odd = jnp.where(low, swap(taken), taken)
    taps[...] = jnp.where(lax.rem(g, 2) == 0, even, odd)

    for copy in h_copies:
        copy.wait_recv()
    slot = {step: i - 2 for i, step in enumerate(h_steps)}
    left, right = 7, 8 + wide
    for r in range(2):
        wx[r + 1, left : left + 1] = hb[slot[0, 1], r, 7:8]
        wx[r + 1, right : right + 1] = hb[slot[0, -1], r, 0:1]
    top = jnp.where(lat > 0, 1.0, 0.0)
    bottom = jnp.where(lat < band_count - 1, 1.0, 0.0)

    def above(low_part, own):
        return jnp.where(low_lanes(own.shape), low_part * top, swap(own))

    def below(own, high_part):
        return jnp.where(low_lanes(own.shape), swap(own), high_part * bottom)

    up = hu[...]
    down = hd[...]
    wx[0, 8 : 8 + half] = above(up, wx[2, 8 : 8 + half])
    wx[0, 8 + half : 8 + wide] = above(swap(up), wx[2, 8 + half : 8 + wide])
    wx[0, left : left + 1] = above(swap(hb[slot[1, 1], 1, 7:8]), wx[2, left : left + 1])
    wx[0, right : right + 1] = above(swap(hb[slot[1, -1], 1, 0:1]), wx[2, right : right + 1])
    wx[3, 8 : 8 + half] = below(wx[1, 8 : 8 + half], swap(down))
    wx[3, 8 + half : 8 + wide] = below(wx[1, 8 + half : 8 + wide], down)
    wx[3, left : left + 1] = below(wx[1, left : left + 1], swap(hb[slot[-1, 1], 0, 7:8]))
    wx[3, right : right + 1] = below(wx[1, right : right + 1], swap(hb[slot[-1, -1], 0, 0:1]))

    for r in range(2):
        value = wx[r + 1, 8 : 8 + wide]
        for a in (-1, 0, 1):
            for b in (-1, 0, 1):
                tap = 3 * (a + 1) + (b + 1)
                value = value + taps[tap : tap + 1] * wx[r + 1 - a, 8 - b : 8 - b + wide]
        high = value.astype(BF16).astype(F32)
        low = value - high
        ro[r] = both_low(high, low).astype(BF16)
        ro[r + 2] = both_high(high, low).astype(BF16)
        o1, o2 = split2(jnp.transpose(value))
        for part in range(2):
            rows = slice(part * HD, (part + 1) * HD)
            for place, piece in enumerate((o1, o2, o1, o2)):
                bd[r + 2 * part, place * HD : (place + 1) * HD] = piece[rows]

    for copy in y_copies:
        copy.wait_recv()
    kv = kvy[...].reshape(keys, 128)
    s1 = kv.astype(BF16).astype(F32)
    rest = kv - s1
    s2 = rest.astype(BF16).astype(F32)
    s3 = rest - s2
    low = low_lanes(kv.shape)
    r1, r2, r3 = swap(s1), swap(s2), swap(s3)
    ak[:, 0:128] = jnp.where(low, s1, r1).astype(BF16)
    ak[:, 128:256] = jnp.where(low, s2, r2).astype(BF16)
    ak[:, 256:384] = jnp.where(low, s1, r3).astype(BF16)
    av[:, 0:128] = jnp.where(low, r1, s1).astype(BF16)
    av[:, 128:256] = jnp.where(low, r2, s2).astype(BF16)
    t1, t2 = split2(jnp.transpose(kv))
    kt[0:HD] = t1[0:HD]
    kt[HD : 2 * HD] = t2[0:HD]
    vt[0:HD] = t1[HD : 2 * HD]
    vt[HD : 2 * HD] = t2[HD : 2 * HD]

    out_parts = []
    query_parts = []
    for r in range(ROWS):
        logits = dot(ak[...], bs[r])
        raised = jnp.exp(logits - jnp.max(logits, 0, keepdims=True))
        soft = raised * (1.0 / jnp.sum(raised, 0, keepdims=True))
        soft_high, soft_low = split2(soft)
        ph[r] = soft_high
        plo[r] = soft_low
        both = dot(vt[...], soft_high) + dot(vt[...], soft_low)
        out_parts.append(both[0:HD] + both[HD : 2 * HD])
        prob_grad = dot(av[...], bd[r])
        row_dot = jnp.sum(soft * prob_grad, 0, keepdims=True)
        grad_high, grad_low = split2(soft * (prob_grad - row_dot))
        dh[r] = grad_high
        dlo[r] = grad_low
        both = dot(kt[...], grad_high) + dot(kt[...], grad_low)
        query_parts.append((both[0:HD] + both[HD : 2 * HD]) * (HD ** -0.5))

    for r in range(2):
        dqs[r] = jnp.transpose(jnp.concatenate([query_parts[r], query_parts[r + 2]], 0))
        op[r] = jnp.transpose(jnp.concatenate([out_parts[r], out_parts[r + 2]], 0))
    d_copies = []
    for e, peer in enumerate(x_peers):
        to = pl.multiple_of(around(g, e + 1, group) * COLS, 8)
        source = dqs.at[:, pl.ds(to, COLS), :]
        d_copies.append(send(source, dqr.at[g], d_s.at[e], d_r.at[e], peer))
    dqr[g] = dqs[:, pl.ds(own_q, COLS), :]

    sums = []
    for a in (-1, 0, 1):
        for b in (-1, 0, 1):
            total = jnp.sum(
                op[0] * wx[1 - a, 8 - b : 8 - b + wide]
                + op[1] * wx[2 - a, 8 - b : 8 - b + wide],
                0,
                keepdims=True,
            )
            sums.append(total + swap(total))
    first = jnp.concatenate(sums[0:8], 0)
    line = lax.broadcasted_iota(jnp.int32, (8, 128), 0)
    last = jnp.where(line == 0, jnp.broadcast_to(sums[8], (8, 128)), 0.0)
    tap_tile = jnp.where(low_lanes((8, 128)), first, last)

    value_terms = dot(ph[0], ro[0]) + dot(plo[0], ro[0])
    key_terms = dot(dh[0], rq[0]) + dot(dlo[0], rq[0])
    for r in range(1, ROWS):
        value_terms = value_terms + dot(ph[r], ro[r]) + dot(plo[r], ro[r])
        key_terms = key_terms + dot(dh[r], rq[r]) + dot(dlo[r], rq[r])
    terms = jnp.where(
        low_lanes(key_terms.shape), key_terms + swap(key_terms), value_terms + swap(value_terms)
    ).reshape(ny, nz, group, 128)
    for i in range(ny):
        dkvb[i, 0:nz, 0:group] = terms[i]
        dkvb[i, nz, 0:8] = tap_tile
    ry_copies = []
    for e, peer in enumerate(y_peers):
        to = around(y, e + 1, ny)
        ry_copies.append(send(dkvb.at[to], rsy.at[y], ry_s.at[e], ry_r.at[e], peer))
    rsy[y] = dkvb[y]
    for copy in ry_copies:
        copy.wait_recv()
    total = rsy[0]
    for i in range(1, ny):
        total = total + rsy[i]
    zs[:, 0] = total[0:nz]
    zs[:, 1] = jnp.broadcast_to(total[nz : nz + 1], (nz, *total.shape[1:]))
    rz_copies = []
    for e, peer in enumerate(z_peers):
        to = around(z, e + 1, nz)
        rz_copies.append(send(zs.at[to], rsz.at[z], rz_s.at[e], rz_r.at[e], peer))
    rsz[z] = zs[z]

    for copy in d_copies:
        copy.wait_recv()
    for m in range(group // 2):
        cut = slice(m * 128, (m + 1) * 128)
        for r in range(2):
            dq_ref[r, :, cut] = both_low(dqr[2 * m, r], dqr[2 * m + 1, r])
            dq_ref[r + 2, :, cut] = both_high(dqr[2 * m, r], dqr[2 * m + 1, r])

    for copy in rz_copies:
        copy.wait_recv()
    total = rsz[0]
    for i in range(1, nz):
        total = total + rsz[i]
    for j in range(group):
        fxs[j] = total[0, j : j + 1]
    txs[...] = total[1]
    fx_copies = []
    tx_copies = []
    for e, peer in enumerate(x_peers):
        to = around(g, e + 1, group)
        fx_copies.append(send(fxs.at[to], fxr.at[g], fx_s.at[e], fx_r.at[e], peer))
        tx_copies.append(send(txs, txr.at[g], tx_s.at[e], tx_r.at[e], peer))
    fxr[g] = fxs[g]
    txr[g] = txs[...]
    for copy in fx_copies + tx_copies:
        copy.wait_recv()
    for m in range(group // 2):
        cut = slice(m * 128, (m + 1) * 128)
        dk_ref[:, cut] = both_low(fxr[2 * m], fxr[2 * m + 1])
        dv_ref[:, cut] = both_high(fxr[2 * m], fxr[2 * m + 1])
    square = txr[0] * txr[0]
    for i in range(1, group):
        square = square + txr[i] * txr[i]
    mean = jnp.sum(square) * (1.0 / (9 * channels))
    scale = jnp.sqrt(jnp.full((8, 128), mean, F32) + 1e-6)
    for m in range(group // 2):
        cut = slice(m * 128, (m + 1) * 128)
        one, two = txr[2 * m, 0:8], txr[2 * m + 1, 0:8]
        tu_ref[0:8, cut] = both_low(one, two) / scale
        tu_ref[8:9, cut] = (both_high(one, two) / scale)[0:1]

    for copies in (
        kx_copies, w_copies, q_copies, z_copies, h_copies, y_copies,
        d_copies, ry_copies, rz_copies, fx_copies, tx_copies,
    ):
        for copy in copies:
            copy.wait_send()


def body(sizes, queries, key_rows, value_rows, cotangent, conv_taps):
    nx, ny, nzl, nzh = sizes
    group = 2 * nx
    nz = nzl * nzh
    wide = group * COLS
    keys = ny * nz * group
    tile = max(group, 8)
    channels = group * HD
    vmem = pltpu.VMEM
    scratch = [
        vmem((group, 2, COLS, 128), F32),
        vmem((group, 2, COLS, 128), F32),
        vmem((4, wide + 16, 128), F32),
        vmem((2, wide, 128), F32),
        vmem((group, 1, 128), F32),
        vmem((group, 1, 128), F32),
        vmem((ny, nz, group, 128), F32),
        vmem((wide // 2, 128), F32),
        vmem((wide // 2, 128), F32),
        vmem((wide // 2, 128), F32),
        vmem((wide // 2, 128), F32),
        vmem((6, 2, 8, 128), F32),
        vmem((16, 128), F32),
        vmem((ROWS, 6 * HD, wide), BF16),
        vmem((ROWS, 4 * HD, wide), BF16),
        vmem((ROWS, wide, 128), BF16),
        vmem((ROWS, wide, 128), BF16),
        vmem((keys, 6 * HD), BF16),
        vmem((keys, 4 * HD), BF16),
        vmem((128, keys), BF16),
        vmem((128, keys), BF16),
        vmem((ROWS, keys, wide), BF16),
        vmem((ROWS, keys, wide), BF16),
        vmem((ROWS, keys, wide), BF16),
        vmem((ROWS, keys, wide), BF16),
        vmem((2, wide, 128), F32),
        vmem((2, wide, 128), F32),
        vmem((group, 2, COLS, 128), F32),
        vmem((ny, nz + 1, tile, 128), F32),
        vmem((ny, nz + 1, tile, 128), F32),
        vmem((nz, 2, tile, 128), F32),
        vmem((nz, 2, tile, 128), F32),
        vmem((group, 1, 128), F32),
        vmem((group, 1, 128), F32),
        vmem((tile, 128), F32),
        vmem((group, tile, 128), F32),
    ]
    counts = (
        group - 1, group - 1, group - 1, nz - 1, ny - 1, 8,
        group - 1, ny - 1, nz - 1, group - 1, group - 1,
    )
    for count in counts:
        scratch += [pltpu.SemaphoreType.DMA((count,)), pltpu.SemaphoreType.DMA((count,))]
    whole = pl.BlockSpec(memory_space=pltpu.VMEM)
    return pl.pallas_call(
        functools.partial(kernel, sizes),
        out_shape=(
            jax.ShapeDtypeStruct((ROWS, COLS, channels), F32),
            jax.ShapeDtypeStruct((1, channels), F32),
            jax.ShapeDtypeStruct((1, channels), F32),
            jax.ShapeDtypeStruct((9, channels), F32),
        ),
        in_specs=[whole] * 5,
        out_specs=(whole,) * 4,
        scratch_shapes=scratch,
        compiler_params=pltpu.CompilerParams(
            collective_id=0, has_side_effects=True, vmem_limit_bytes=48 << 20
        ),
    )(queries, cotangent, key_rows, value_rows, conv_taps)


def solution(mesh):
    sizes = (NX, NY, mesh.shape["lon"] // (2 * NX), mesh.shape["lat"] // NY)
    placed = (
        P("lat", "lon", None),
        P(("lat", "lon"), None),
        P(("lat", "lon"), None),
        P("lat", "lon", None),
        P(),
    )
    return jax.shard_map(
        functools.partial(body, sizes),
        mesh=mesh,
        in_specs=placed,
        out_specs=(P("lat", "lon", None), P(("lat", "lon"), None), P(("lat", "lon"), None), P()),
        check_vma=False,
    )
```

```python
import functools

import jax
import jax.numpy as jnp
import numpy as np
from jax import lax
from jax.experimental import pallas as pl
from jax.experimental.pallas import tpu as pltpu
from jax.sharding import PartitionSpec as P

HD = 64
NX = 4
NY = 4
ROWS = 4
COLS = 32
F32 = jnp.float32
BF16 = jnp.bfloat16
MESH = pl.DeviceIdType.MESH


def low_lanes(shape):
    return lax.broadcasted_iota(jnp.int32, shape, len(shape) - 1) < HD


def swap(value):
    return pltpu.roll(value, HD, value.ndim - 1)


def both_low(first, second):
    return jnp.where(low_lanes(first.shape), first, swap(second))


def both_high(first, second):
    return jnp.where(low_lanes(first.shape), swap(first), second)


def split2(value):
    high = value.astype(BF16)
    return high, (value - high.astype(F32)).astype(BF16)


def split3(value):
    first = value.astype(BF16)
    rest = value - first.astype(F32)
    second = rest.astype(BF16)
    return first, second, (rest - second.astype(F32)).astype(BF16)


def dot(a, b):
    return jnp.dot(a, b, preferred_element_type=F32)


def kernel(
    sizes,
    q_hbm, c_hbm, k_hbm, v_hbm, t_hbm,
    dq_ref, dk_ref, dv_ref, tu_ref,
    q_ref, c_ref, k_ref, v_ref, t_ref, in_s,
    ws, qs, wx, qx, kvs, kvx, kvy, hus, hds, hu, hd, hb,
    taps, bs, bd, rq, ro, ak, av, kt, vt, pf, ph, plo, dh, dlo, op, dqs, dqr,
    dkvb, rsy, zs, rsz, fxs, fxr, txs, txr, tys, tyr, tzs, tzr,
    w_s, w_r, q_s, q_r, kx_s, kx_r, z_s, z_r, y_s, y_r, h_s, h_r,
    d_s, d_r, ry_s, ry_r, rz_s, rz_r, fx_s, fx_r, tx_s, tx_r, ty_s, ty_r, tz_s, tz_r,
):
    nx, ny, nzl, nzh = sizes
    group = 2 * nx
    nz = nzl * nzh
    band_count = nzh * ny
    wide = group * COLS
    keys = ny * nz * group
    channels = group * HD
    lat = lax.axis_index("lat")
    lon = lax.axis_index("lon")
    y = lax.rem(lat, ny)
    z_hi = lax.div(lat, ny)
    z_lo = lax.div(lon, group)
    g = lax.rem(lon, group)
    z = z_hi * nzl + z_lo

    def at(z_of, y_of, g_of):
        return (lax.div(z_of, nzl) * ny + y_of, lax.rem(z_of, nzl) * group + g_of)

    def around(value, step, count):
        return lax.rem(value + step + count, count)

    x_peers = [at(z, y, around(g, e, group)) for e in range(1, group)]
    z_steps = sorted(range(1, nz), key=lambda e: -min(e, nz - e))
    z_peers = [at(around(z, e, nz), y, g) for e in z_steps]
    y_peers = [at(z, around(y, e, ny), g) for e in range(1, ny)]

    def beside(d_lat, d_lon):
        return (around(lat, d_lat, band_count), around(z_lo, d_lon, nzl) * group + g)

    h_steps = [(1, 0), (-1, 0)] + [(a, b) for a in (-1, 0, 1) for b in (1, -1)]
    h_peers = [beside(a, b) for a, b in h_steps]

    barrier = pltpu.get_barrier_semaphore()
    inputs = []
    for i, (source, target) in enumerate(
        ((k_hbm, k_ref), (v_hbm, v_ref), (c_hbm, c_ref), (q_hbm, q_ref), (t_hbm, t_ref))
    ):
        inputs.append(pltpu.make_async_copy(source, target, in_s.at[i]))
        inputs[i].start()
    partners = x_peers + z_peers + y_peers + h_peers
    for peer in partners:
        pl.semaphore_signal(barrier, inc=1, device_id=peer, device_id_type=MESH)

    def send(source, target, send_sem, recv_sem, peer):
        copy = pltpu.make_async_remote_copy(
            src_ref=source, dst_ref=target, send_sem=send_sem, recv_sem=recv_sem,
            device_id=peer, device_id_type=MESH,
        )
        copy.start()
        started.append(copy)
        return copy

    started = []
    arrived = []

    def arrive(copies):
        for copy in copies:
            copy.wait_recv()
            arrived.append(copy)

    inputs[0].wait()
    inputs[1].wait()
    for m in range(group // 2):
        cut = slice(m * 128, (m + 1) * 128)
        k_part = k_ref[:, cut]
        v_part = v_ref[:, cut]
        kvs[2 * m] = both_low(k_part, v_part)
        kvs[2 * m + 1] = both_high(k_part, v_part)
    own_w = pl.multiple_of(8 + COLS * g, 8)
    own_q = pl.multiple_of(COLS * g, 8)

    pl.semaphore_wait(barrier, len(partners))

    kx_copies = []
    for e, peer in enumerate(x_peers):
        to = around(g, e + 1, group)
        kx_copies.append(send(kvs.at[to], kvx.at[g], kx_s.at[e], kx_r.at[e], peer))
    kvx[g] = kvs[g]
    inputs[2].wait()
    line_total = ROWS * band_count
    centres = (np.arange(line_total) + 0.5) * np.pi / line_total
    mean_cosine = float(np.mean(np.sin(centres)))
    line = lax.broadcasted_iota(jnp.int32, (8, 128), 0) + lat * ROWS
    weight = jnp.sin((line.astype(F32) + 0.5) * (np.pi / line_total)) / mean_cosine
    for m in range(group // 2):
        cut = slice(m * 128, (m + 1) * 128)
        for r in range(2):
            upper = c_ref[r, :, cut] * weight[r : r + 1]
            lower = c_ref[r + 2, :, cut] * weight[r + 2 : r + 3]
            ws[2 * m, r] = both_low(upper, lower)
            ws[2 * m + 1, r] = both_high(upper, lower)
    w_copies = []
    for e, peer in enumerate(x_peers):
        to = around(g, e + 1, group)
        target = wx.at[pl.ds(1, 2), pl.ds(own_w, COLS), :]
        w_copies.append(send(ws.at[to], target, w_s.at[e], w_r.at[e], peer))
    wx[pl.ds(1, 2), pl.ds(own_w, COLS), :] = ws[g]
    inputs[3].wait()
    for m in range(group // 2):
        cut = slice(m * 128, (m + 1) * 128)
        for r in range(2):
            upper = q_ref[r, :, cut] * (HD ** -0.5)
            lower = q_ref[r + 2, :, cut] * (HD ** -0.5)
            qs[2 * m, r] = both_low(upper, lower)
            qs[2 * m + 1, r] = both_high(upper, lower)
    q_copies = []
    for e, peer in enumerate(x_peers):
        to = around(g, e + 1, group)
        target = qx.at[:, pl.ds(own_q, COLS), :]
        q_copies.append(send(qs.at[to], target, q_s.at[e], q_r.at[e], peer))
    qx[:, pl.ds(own_q, COLS), :] = qs[g]

    arrive(kx_copies)
    kvy[y, z] = jnp.concatenate([kvx[j] for j in range(group)], 0)
    z_copies = []
    for e, peer in enumerate(z_peers):
        z_copies.append(send(kvy.at[y, z], kvy.at[y, z], z_s.at[e], z_r.at[e], peer))

    arrive(w_copies)
    half = wide // 2
    hus[...] = both_high(wx[2, 8 : 8 + half], wx[2, 8 + half : 8 + wide])
    hds[...] = both_low(wx[1, 8 : 8 + half], wx[1, 8 + half : 8 + wide])
    h_copies = []
    for i, (a, b) in enumerate(h_steps):
        if b == 0:
            source, target = (hus, hu) if a == 1 else (hds, hd)
        else:
            source = wx.at[pl.ds(1, 2), pl.ds(wide if b == 1 else 8, 8), :]
            target = hb.at[i - 2]
        h_copies.append(send(source, target, h_s.at[i], h_r.at[i], h_peers[i]))

    arrive(q_copies)
    for r in range(2):
        value = qx[r]
        high = value.astype(BF16).astype(F32)
        low = value - high
        rq[r] = both_low(high, low).astype(BF16)
        rq[r + 2] = both_high(high, low).astype(BF16)
        q1, q2, q3 = split3(jnp.transpose(value))
        for part in range(2):
            rows = slice(part * HD, (part + 1) * HD)
            for place, piece in enumerate((q1, q2, q1, q2, q3, q1)):
                bs[r + 2 * part, place * HD : (place + 1) * HD] = piece[rows]

    arrive(z_copies)
    y_copies = []
    for e, peer in enumerate(y_peers):
        y_copies.append(send(kvy.at[y], kvy.at[y], y_s.at[e], y_r.at[e], peer))

    pair = pl.multiple_of(lax.div(g, 2) * 128, 128)
    inputs[4].wait()
    taps[0:9] = t_ref[:, pl.ds(pair, 128)]
    taken = taps[...]
    low = low_lanes(taken.shape)
    even = jnp.where(low, taken, swap(taken))
    odd = jnp.where(low, swap(taken), taken)
    taps[...] = jnp.where(lax.rem(g, 2) == 0, even, odd)

    arrive(y_copies)
    kv = kvy[...].reshape(keys, 128)
    s1 = kv.astype(BF16).astype(F32)
    rest = kv - s1
    s2 = rest.astype(BF16).astype(F32)
    s3 = rest - s2
    low = low_lanes(kv.shape)
    r1, r2, r3 = swap(s1), swap(s2), swap(s3)
    ak[:, 0:128] = jnp.where(low, s1, r1).astype(BF16)
    ak[:, 128:256] = jnp.where(low, s2, r2).astype(BF16)
    ak[:, 256:384] = jnp.where(low, s1, r3).astype(BF16)
    av[:, 0:128] = jnp.where(low, r1, s1).astype(BF16)
    av[:, 128:256] = jnp.where(low, r2, s2).astype(BF16)
    t1, t2 = split2(jnp.transpose(kv))
    kt[0:HD] = t1[0:HD]
    kt[HD : 2 * HD] = t2[0:HD]
    vt[0:HD] = t1[HD : 2 * HD]
    vt[HD : 2 * HD] = t2[HD : 2 * HD]

    out_parts = []
    for r in range(ROWS):
        logits = dot(ak[...], bs[r])
        raised = jnp.exp(logits - jnp.max(logits, 0, keepdims=True))
        soft = raised * (1.0 / jnp.sum(raised, 0, keepdims=True))
        soft_high, soft_low = split2(soft)
        pf[r] = soft
        ph[r] = soft_high
        plo[r] = soft_low
        both = dot(vt[...], soft_high) + dot(vt[...], soft_low)
        out_parts.append(both[0:HD] + both[HD : 2 * HD])
    for r in range(2):
        op[r] = jnp.transpose(jnp.concatenate([out_parts[r], out_parts[r + 2]], 0))

    arrive(h_copies)
    slot = {step: i - 2 for i, step in enumerate(h_steps)}
    left, right = 7, 8 + wide
    for r in range(2):
        wx[r + 1, left : left + 1] = hb[slot[0, 1], r, 7:8]
        wx[r + 1, right : right + 1] = hb[slot[0, -1], r, 0:1]
    top = jnp.where(lat > 0, 1.0, 0.0)
    bottom = jnp.where(lat < band_count - 1, 1.0, 0.0)

    def above(low_part, own):
        return jnp.where(low_lanes(own.shape), low_part * top, swap(own))

    def below(own, high_part):
        return jnp.where(low_lanes(own.shape), swap(own), high_part * bottom)

    up = hu[...]
    down = hd[...]
    wx[0, 8 : 8 + half] = above(up, wx[2, 8 : 8 + half])
    wx[0, 8 + half : 8 + wide] = above(swap(up), wx[2, 8 + half : 8 + wide])
    wx[0, left : left + 1] = above(swap(hb[slot[1, 1], 1, 7:8]), wx[2, left : left + 1])
    wx[0, right : right + 1] = above(swap(hb[slot[1, -1], 1, 0:1]), wx[2, right : right + 1])
    wx[3, 8 : 8 + half] = below(wx[1, 8 : 8 + half], swap(down))
    wx[3, 8 + half : 8 + wide] = below(wx[1, 8 + half : 8 + wide], down)
    wx[3, left : left + 1] = below(wx[1, left : left + 1], swap(hb[slot[-1, 1], 0, 7:8]))
    wx[3, right : right + 1] = below(wx[1, right : right + 1], swap(hb[slot[-1, -1], 0, 0:1]))

    for r in range(2):
        value = wx[r + 1, 8 : 8 + wide]
        for a in (-1, 0, 1):
            for b in (-1, 0, 1):
                tap = 3 * (a + 1) + (b + 1)
                value = value + taps[tap : tap + 1] * wx[r + 1 - a, 8 - b : 8 - b + wide]
        high = value.astype(BF16).astype(F32)
        low = value - high
        ro[r] = both_low(high, low).astype(BF16)
        ro[r + 2] = both_high(high, low).astype(BF16)
        o1, o2 = split2(jnp.transpose(value))
        for part in range(2):
            rows = slice(part * HD, (part + 1) * HD)
            for place, piece in enumerate((o1, o2, o1, o2)):
                bd[r + 2 * part, place * HD : (place + 1) * HD] = piece[rows]

    sums = []
    for a in (-1, 0, 1):
        for b in (-1, 0, 1):
            total = jnp.sum(
                op[0] * wx[1 - a, 8 - b : 8 - b + wide]
                + op[1] * wx[2 - a, 8 - b : 8 - b + wide],
                0,
                keepdims=True,
            )
            sums.append(total + swap(total))
    first = jnp.concatenate(sums[0:8], 0)
    line = lax.broadcasted_iota(jnp.int32, (8, 128), 0)
    last = jnp.where(line == 0, jnp.broadcast_to(sums[8], (8, 128)), 0.0)
    tap_tile = jnp.where(low_lanes((8, 128)), first, last)

    tys[...] = tap_tile
    ty_copies = []
    for e, peer in enumerate(y_peers):
        ty_copies.append(send(tys, tyr.at[y], ty_s.at[e], ty_r.at[e], peer))
    tyr[y] = tap_tile

    query_parts = []
    for r in range(ROWS):
        soft = pf[r]
        prob_grad = dot(av[...], bd[r])
        row_dot = jnp.sum(soft * prob_grad, 0, keepdims=True)
        grad_high, grad_low = split2(soft * (prob_grad - row_dot))
        dh[r] = grad_high
        dlo[r] = grad_low
        both = dot(kt[...], grad_high) + dot(kt[...], grad_low)
        query_parts.append((both[0:HD] + both[HD : 2 * HD]) * (HD ** -0.5))

    for r in range(2):
        dqs[r] = jnp.transpose(jnp.concatenate([query_parts[r], query_parts[r + 2]], 0))
    d_copies = []
    for e, peer in enumerate(x_peers):
        to = pl.multiple_of(around(g, e + 1, group) * COLS, 8)
        source = dqs.at[:, pl.ds(to, COLS), :]
        d_copies.append(send(source, dqr.at[g], d_s.at[e], d_r.at[e], peer))
    dqr[g] = dqs[:, pl.ds(own_q, COLS), :]

    arrive(ty_copies)
    total = tyr[0]
    for i in range(1, ny):
        total = total + tyr[i]
    tzs[...] = total
    tz_copies = []
    for e, peer in enumerate(z_peers):
        tz_copies.append(send(tzs, tzr.at[z], tz_s.at[e], tz_r.at[e], peer))
    tzr[z] = total

    value_terms = dot(ph[0], ro[0]) + dot(plo[0], ro[0])
    key_terms = dot(dh[0], rq[0]) + dot(dlo[0], rq[0])
    for r in range(1, ROWS):
        value_terms = value_terms + dot(ph[r], ro[r]) + dot(plo[r], ro[r])
        key_terms = key_terms + dot(dh[r], rq[r]) + dot(dlo[r], rq[r])
    terms = jnp.where(
        low_lanes(key_terms.shape), key_terms + swap(key_terms), value_terms + swap(value_terms)
    ).reshape(ny, nz, group, 128)
    for i in range(ny):
        dkvb[i] = terms[i]
    ry_copies = []
    for e, peer in enumerate(y_peers):
        to = around(y, e + 1, ny)
        ry_copies.append(send(dkvb.at[to], rsy.at[y], ry_s.at[e], ry_r.at[e], peer))
    rsy[y] = dkvb[y]
    arrive(ry_copies)
    total = rsy[0]
    for i in range(1, ny):
        total = total + rsy[i]
    zs[...] = total
    rz_copies = []
    for e, peer in enumerate(z_peers):
        to = around(z, z_steps[e], nz)
        rz_copies.append(send(zs.at[to], rsz.at[z], rz_s.at[e], rz_r.at[e], peer))
    rsz[z] = zs[z]

    arrive(tz_copies)
    total = tzr[0]
    for i in range(1, nz):
        total = total + tzr[i]
    txs[...] = total
    tx_copies = []
    for e, peer in enumerate(x_peers):
        tx_copies.append(send(txs, txr.at[g], tx_s.at[e], tx_r.at[e], peer))
    txr[g] = total

    arrive(d_copies)
    for m in range(group // 2):
        cut = slice(m * 128, (m + 1) * 128)
        for r in range(2):
            dq_ref[r, :, cut] = both_low(dqr[2 * m, r], dqr[2 * m + 1, r])
            dq_ref[r + 2, :, cut] = both_high(dqr[2 * m, r], dqr[2 * m + 1, r])

    arrive(rz_copies)
    total = rsz[0]
    for i in range(1, nz):
        total = total + rsz[i]
    for j in range(group):
        fxs[j] = total[j : j + 1]
    fx_copies = []
    for e, peer in enumerate(x_peers):
        to = around(g, e + 1, group)
        fx_copies.append(send(fxs.at[to], fxr.at[g], fx_s.at[e], fx_r.at[e], peer))
    fxr[g] = fxs[g]

    arrive(tx_copies)
    square = txr[0] * txr[0]
    for i in range(1, group):
        square = square + txr[i] * txr[i]
    mean = jnp.sum(square) * (1.0 / (9 * channels))
    scale = jnp.sqrt(jnp.full((8, 128), mean, F32) + 1e-6)
    for m in range(group // 2):
        cut = slice(m * 128, (m + 1) * 128)
        one, two = txr[2 * m, 0:8], txr[2 * m + 1, 0:8]
        tu_ref[0:8, cut] = both_low(one, two) / scale
        tu_ref[8:9, cut] = (both_high(one, two) / scale)[0:1]

    arrive(fx_copies)
    for m in range(group // 2):
        cut = slice(m * 128, (m + 1) * 128)
        dk_ref[:, cut] = both_low(fxr[2 * m], fxr[2 * m + 1])
        dv_ref[:, cut] = both_high(fxr[2 * m], fxr[2 * m + 1])
    for copy in started:
        copy.wait_send()


def body(sizes, queries, key_rows, value_rows, cotangent, conv_taps):
    nx, ny, nzl, nzh = sizes
    group = 2 * nx
    nz = nzl * nzh
    wide = group * COLS
    keys = ny * nz * group
    channels = group * HD
    vmem = pltpu.VMEM
    scratch = [
        vmem((ROWS, COLS, channels), F32),
        vmem((ROWS, COLS, channels), F32),
        vmem((1, channels), F32),
        vmem((1, channels), F32),
        vmem((9, channels), F32),
        pltpu.SemaphoreType.DMA((5,)),
        vmem((group, 2, COLS, 128), F32),
        vmem((group, 2, COLS, 128), F32),
        vmem((4, wide + 16, 128), F32),
        vmem((2, wide, 128), F32),
        vmem((group, 1, 128), F32),
        vmem((group, 1, 128), F32),
        vmem((ny, nz, group, 128), F32),
        vmem((wide // 2, 128), F32),
        vmem((wide // 2, 128), F32),
        vmem((wide // 2, 128), F32),
        vmem((wide // 2, 128), F32),
        vmem((6, 2, 8, 128), F32),
        vmem((16, 128), F32),
        vmem((ROWS, 6 * HD, wide), BF16),
        vmem((ROWS, 4 * HD, wide), BF16),
        vmem((ROWS, wide, 128), BF16),
        vmem((ROWS, wide, 128), BF16),
        vmem((keys, 6 * HD), BF16),
        vmem((keys, 4 * HD), BF16),
        vmem((128, keys), BF16),
        vmem((128, keys), BF16),
        vmem((ROWS, keys, wide), F32),
        vmem((ROWS, keys, wide), BF16),
        vmem((ROWS, keys, wide), BF16),
        vmem((ROWS, keys, wide), BF16),
        vmem((ROWS, keys, wide), BF16),
        vmem((2, wide, 128), F32),
        vmem((2, wide, 128), F32),
        vmem((group, 2, COLS, 128), F32),
        vmem((ny, nz, group, 128), F32),
        vmem((ny, nz, group, 128), F32),
        vmem((nz, group, 128), F32),
        vmem((nz, group, 128), F32),
        vmem((group, 1, 128), F32),
        vmem((group, 1, 128), F32),
        vmem((8, 128), F32),
        vmem((group, 8, 128), F32),
        vmem((8, 128), F32),
        vmem((ny, 8, 128), F32),
        vmem((8, 128), F32),
        vmem((nz, 8, 128), F32),
    ]
    counts = (
        group - 1, group - 1, group - 1, nz - 1, ny - 1, 8,
        group - 1, ny - 1, nz - 1, group - 1, group - 1, ny - 1, nz - 1,
    )
    for count in counts:
        scratch += [pltpu.SemaphoreType.DMA((count,)), pltpu.SemaphoreType.DMA((count,))]
    whole = pl.BlockSpec(memory_space=pltpu.VMEM)
    return pl.pallas_call(
        functools.partial(kernel, sizes),
        out_shape=(
            jax.ShapeDtypeStruct((ROWS, COLS, channels), F32),
            jax.ShapeDtypeStruct((1, channels), F32),
            jax.ShapeDtypeStruct((1, channels), F32),
            jax.ShapeDtypeStruct((9, channels), F32),
        ),
        in_specs=[pl.BlockSpec(memory_space=pltpu.HBM)] * 5,
        out_specs=(whole,) * 4,
        scratch_shapes=scratch,
        compiler_params=pltpu.CompilerParams(
            collective_id=0, has_side_effects=True, vmem_limit_bytes=48 << 20
        ),
    )(queries, cotangent, key_rows, value_rows, conv_taps)


def solution(mesh):
    sizes = (NX, NY, mesh.shape["lon"] // (2 * NX), mesh.shape["lat"] // NY)
    placed = (
        P("lat", "lon", None),
        P(("lat", "lon"), None),
        P(("lat", "lon"), None),
        P("lat", "lon", None),
        P(),
    )
    return jax.shard_map(
        functools.partial(body, sizes),
        mesh=mesh,
        in_specs=placed,
        out_specs=(P("lat", "lon", None), P(("lat", "lon"), None), P(("lat", "lon"), None), P()),
        check_vma=False,
    )
```

```python
import functools

import jax
import jax.numpy as jnp
import numpy as np
from jax import lax
from jax.experimental import pallas as pl
from jax.experimental.pallas import tpu as pltpu
from jax.sharding import PartitionSpec as P

HD = 64
NX = 4
NY = 4
ROWS = 4
COLS = 32
F32 = jnp.float32
BF16 = jnp.bfloat16
MESH = pl.DeviceIdType.MESH


def low_lanes(shape):
    return lax.broadcasted_iota(jnp.int32, shape, len(shape) - 1) < HD


def swap(value):
    return pltpu.roll(value, HD, value.ndim - 1)


def both_low(first, second):
    return jnp.where(low_lanes(first.shape), first, swap(second))


def both_high(first, second):
    return jnp.where(low_lanes(first.shape), swap(first), second)


def split2(value):
    high = value.astype(BF16)
    return high, (value - high.astype(F32)).astype(BF16)


def split3(value):
    first = value.astype(BF16)
    rest = value - first.astype(F32)
    second = rest.astype(BF16)
    return first, second, (rest - second.astype(F32)).astype(BF16)


def dot(a, b):
    return jnp.dot(a, b, preferred_element_type=F32)


def kernel(
    sizes,
    q_hbm, c_hbm, k_hbm, v_hbm, t_hbm,
    dq_ref, dk_ref, dv_ref, tu_ref,
    q_ref, c_ref, k_ref, v_ref, t_ref, in_s,
    ws, qs, wx, qx, kvz, ks, vs, kp, vp, hus, hds, hu, hd, hb,
    taps, bs, bd, rq, ro, ak, av, kt, vt, pf, ph, plo, dh, dlo, op, dqs, dqr,
    dvb, dkb, dvr, dkr, dvt, dkt, zs, rsz, tzs, tzr, txs, txr,
    w_s, w_r, q_s, q_r, z_s, z_r, k_s, k_r, v_s, v_r, u_s, u_r, n_s, n_r, h_s, h_r,
    d_s, d_r, rv_s, rv_r, rk_s, rk_r, rz_s, rz_r, tz_s, tz_r, tx_s, tx_r,
):
    nx, ny, nzl, nzh = sizes
    group = 2 * nx
    nz = nzl * nzh
    band_count = nzh * ny
    wide = group * COLS
    pairs = nz // 2
    keys_half = ny * group * pairs
    channels = group * HD
    lat = lax.axis_index("lat")
    lon = lax.axis_index("lon")
    y = lax.rem(lat, ny)
    z_hi = lax.div(lat, ny)
    z_lo = lax.div(lon, group)
    g = lax.rem(lon, group)
    z = z_hi * nzl + z_lo

    def at(z_of, y_of, g_of):
        return (lax.div(z_of, nzl) * ny + y_of, lax.rem(z_of, nzl) * group + g_of)

    def around(value, step, count):
        return lax.rem(value + step + count, count)

    x_peers = [at(z, y, around(g, e, group)) for e in range(1, group)]
    z_steps = sorted(range(1, nz), key=lambda e: -min(e, nz - e))
    z_peers = [at(around(z, e, nz), y, g) for e in z_steps]
    far = [(a, b) for a in range(ny) for b in range(group) if a or b]
    far = sorted(far, key=lambda s: -min(s[0], ny - s[0]) - min(s[1], group - s[1]) / 2)
    f_peers = [at(z, around(y, a, ny), around(g, b, group)) for a, b in far]

    def beside(d_lat, d_lon, to):
        return (around(lat, d_lat, band_count), around(z_lo, d_lon, nzl) * group + to)

    u_peers = [beside(1, 0, around(g, e, group)) for e in range(group)]
    n_peers = [beside(-1, 0, around(g, e, group)) for e in range(group)]
    h_steps = [(a, b) for a in (-1, 0, 1) for b in (1, -1)]
    h_peers = [beside(a, b, g) for a, b in h_steps]

    barrier = pltpu.get_barrier_semaphore()
    inputs = []
    for i, (source, target) in enumerate(
        ((k_hbm, k_ref), (v_hbm, v_ref), (c_hbm, c_ref), (q_hbm, q_ref), (t_hbm, t_ref))
    ):
        inputs.append(pltpu.make_async_copy(source, target, in_s.at[i]))
        inputs[i].start()
    partners = f_peers + z_peers + u_peers + n_peers + h_peers
    for peer in partners:
        pl.semaphore_signal(barrier, inc=1, device_id=peer, device_id_type=MESH)

    def send(source, target, send_sem, recv_sem, peer):
        copy = pltpu.make_async_remote_copy(
            src_ref=source, dst_ref=target, send_sem=send_sem, recv_sem=recv_sem,
            device_id=peer, device_id_type=MESH,
        )
        copy.start()
        started.append(copy)
        return copy

    started = []
    arrived = []

    def arrive(copies):
        for copy in copies:
            copy.wait_recv()
            arrived.append(copy)

    inputs[0].wait()
    inputs[1].wait()
    rows = []
    for m in range(group // 2):
        cut = slice(m * 128, (m + 1) * 128)
        rows.append(both_low(k_ref[:, cut], v_ref[:, cut]))
        rows.append(both_high(k_ref[:, cut], v_ref[:, cut]))
    own_z = pl.ds(pl.multiple_of(z * group, group), group)
    kvz[own_z] = jnp.concatenate(rows, 0)
    own_w = pl.multiple_of(8 + COLS * g, 8)
    own_q = pl.multiple_of(COLS * g, 8)

    pl.semaphore_wait(barrier, len(partners))

    z_copies = []
    for e, peer in enumerate(z_peers):
        z_copies.append(send(kvz.at[own_z], kvz.at[own_z], z_s.at[e], z_r.at[e], peer))

    inputs[2].wait()
    line_total = ROWS * band_count
    centres = (np.arange(line_total) + 0.5) * np.pi / line_total
    mean_cosine = float(np.mean(np.sin(centres)))
    line = lax.broadcasted_iota(jnp.int32, (8, 128), 0) + lat * ROWS
    weight = jnp.sin((line.astype(F32) + 0.5) * (np.pi / line_total)) / mean_cosine
    for m in range(group // 2):
        cut = slice(m * 128, (m + 1) * 128)
        for r in range(2):
            upper = c_ref[r, :, cut] * weight[r : r + 1]
            lower = c_ref[r + 2, :, cut] * weight[r + 2 : r + 3]
            ws[2 * m, r] = both_low(upper, lower)
            ws[2 * m + 1, r] = both_high(upper, lower)
            if r == 0:
                hds[2 * m] = both_low(upper[: COLS // 2], upper[COLS // 2 :])
                hds[2 * m + 1] = both_high(upper[: COLS // 2], upper[COLS // 2 :])
            else:
                hus[2 * m] = both_low(lower[: COLS // 2], lower[COLS // 2 :])
                hus[2 * m + 1] = both_high(lower[: COLS // 2], lower[COLS // 2 :])
    u_copies = []
    n_copies = []
    for e in range(group):
        to = around(g, e, group)
        u_copies.append(send(hus.at[to], hu.at[g], u_s.at[e], u_r.at[e], u_peers[e]))
        n_copies.append(send(hds.at[to], hd.at[g], n_s.at[e], n_r.at[e], n_peers[e]))
    w_copies = []
    for e, peer in enumerate(x_peers):
        to = around(g, e + 1, group)
        target = wx.at[pl.ds(1, 2), pl.ds(own_w, COLS), :]
        w_copies.append(send(ws.at[to], target, w_s.at[e], w_r.at[e], peer))
    wx[pl.ds(1, 2), pl.ds(own_w, COLS), :] = ws[g]
    inputs[3].wait()
    for m in range(group // 2):
        cut = slice(m * 128, (m + 1) * 128)
        for r in range(2):
            upper = q_ref[r, :, cut] * (HD ** -0.5)
            lower = q_ref[r + 2, :, cut] * (HD ** -0.5)
            qs[2 * m, r] = both_low(upper, lower)
            qs[2 * m + 1, r] = both_high(upper, lower)
    q_copies = []
    for e, peer in enumerate(x_peers):
        to = around(g, e + 1, group)
        target = qx.at[:, pl.ds(own_q, COLS), :]
        q_copies.append(send(qs.at[to], target, q_s.at[e], q_r.at[e], peer))
    qx[:, pl.ds(own_q, COLS), :] = qs[g]

    arrive(z_copies)
    for h in range(group):
        first = kvz[pl.ds(h, pairs, stride=group)]
        second = kvz[pl.ds(h + group * pairs, pairs, stride=group)]
        ks[h] = both_low(first, second)
        vs[h] = both_high(first, second)
    k_copies = []
    for e, peer in enumerate(f_peers):
        to = around(g, far[e][1], group)
        k_copies.append(send(ks.at[to], kp.at[y, g], k_s.at[e], k_r.at[e], peer))
    v_copies = []
    for e, peer in enumerate(f_peers):
        to = around(g, far[e][1], group)
        v_copies.append(send(vs.at[to], vp.at[y, g], v_s.at[e], v_r.at[e], peer))
    kp[y, g] = ks[g]
    vp[y, g] = vs[g]

    arrive(w_copies)
    h_copies = []
    for i, (a, b) in enumerate(h_steps):
        source = wx.at[pl.ds(1, 2), pl.ds(wide if b == 1 else 8, 8), :]
        h_copies.append(send(source, hb.at[i], h_s.at[i], h_r.at[i], h_peers[i]))

    arrive(q_copies)
    for r in range(2):
        value = qx[r]
        high = value.astype(BF16).astype(F32)
        low = value - high
        rq[r] = both_low(high, low).astype(BF16)
        rq[r + 2] = both_high(high, low).astype(BF16)
        q1, q2, q3 = split3(jnp.transpose(value))
        for part in range(2):
            rows = slice(part * HD, (part + 1) * HD)
            for place, piece in enumerate((q1, q2, q1, q2, q3, q1)):
                bs[r + 2 * part, place * HD : (place + 1) * HD] = piece[rows]

    pair = pl.multiple_of(lax.div(g, 2) * 128, 128)
    inputs[4].wait()
    taps[0:9] = t_ref[:, pl.ds(pair, 128)]
    taken = taps[...]
    low = low_lanes(taken.shape)
    even = jnp.where(low, taken, swap(taken))
    odd = jnp.where(low, swap(taken), taken)
    taps[...] = jnp.where(lax.rem(g, 2) == 0, even, odd)

    def wide_pieces(value):
        s1 = value.astype(BF16).astype(F32)
        rest = value - s1
        s2 = rest.astype(BF16).astype(F32)
        s3 = rest - s2
        low = low_lanes(value.shape)

        def both(a, b):
            first = jnp.where(low, a, swap(b)).astype(BF16)
            return first, jnp.where(low, swap(a), b).astype(BF16)

        return both(s1, s1), both(s2, s2), both(s1, s3)

    def turned_pieces(value, target):
        for i, piece in enumerate(split2(jnp.transpose(value))):
            target[i * HD : (i + 1) * HD, 0:keys_half] = piece[0:HD]
            target[i * HD : (i + 1) * HD, keys_half : 2 * keys_half] = piece[HD : 2 * HD]

    arrive(k_copies)
    value = kp[...].reshape(keys_half, 128)
    for i, (first, second) in enumerate(wide_pieces(value)):
        ak[0:keys_half, i * 128 : (i + 1) * 128] = first
        ak[keys_half : 2 * keys_half, i * 128 : (i + 1) * 128] = second
    turned_pieces(value, kt)

    out_parts = []
    for r in range(ROWS):
        logits = dot(ak[...], bs[r])
        raised = jnp.exp(logits - jnp.max(logits, 0, keepdims=True))
        soft = raised * (1.0 / jnp.sum(raised, 0, keepdims=True))
        soft_high, soft_low = split2(soft)
        pf[r] = soft
        ph[r] = soft_high
        plo[r] = soft_low

    arrive(v_copies)
    value = vp[...].reshape(keys_half, 128)
    for i, (first, second) in enumerate(wide_pieces(value)[0:2]):
        av[0:keys_half, i * 128 : (i + 1) * 128] = first
        av[keys_half : 2 * keys_half, i * 128 : (i + 1) * 128] = second
    turned_pieces(value, vt)
    for r in range(ROWS):
        both = dot(vt[...], ph[r]) + dot(vt[...], plo[r])
        out_parts.append(both[0:HD] + both[HD : 2 * HD])
    for r in range(2):
        op[r] = jnp.transpose(jnp.concatenate([out_parts[r], out_parts[r + 2]], 0))

    arrive(h_copies + u_copies + n_copies)
    slot = {step: i for i, step in enumerate(h_steps)}
    left, right = 7, 8 + wide
    for r in range(2):
        wx[r + 1, left : left + 1] = hb[slot[0, 1], r, 7:8]
        wx[r + 1, right : right + 1] = hb[slot[0, -1], r, 0:1]
    top = jnp.where(lat > 0, 1.0, 0.0)
    bottom = jnp.where(lat < band_count - 1, 1.0, 0.0)

    def above(low_part, own):
        return jnp.where(low_lanes(own.shape), low_part * top, swap(own))

    def below(own, high_part):
        return jnp.where(low_lanes(own.shape), swap(own), high_part * bottom)

    part = COLS // 2
    for j in range(group):
        one = slice(8 + COLS * j, 8 + COLS * j + part)
        two = slice(8 + COLS * j + part, 8 + COLS * (j + 1))
        wx[0, one] = above(hu[j], wx[2, one])
        wx[0, two] = above(swap(hu[j]), wx[2, two])
        wx[3, one] = below(wx[1, one], swap(hd[j]))
        wx[3, two] = below(wx[1, two], hd[j])
    wx[0, left : left + 1] = above(swap(hb[slot[1, 1], 1, 7:8]), wx[2, left : left + 1])
    wx[0, right : right + 1] = above(swap(hb[slot[1, -1], 1, 0:1]), wx[2, right : right + 1])
    wx[3, left : left + 1] = below(wx[1, left : left + 1], swap(hb[slot[-1, 1], 0, 7:8]))
    wx[3, right : right + 1] = below(wx[1, right : right + 1], swap(hb[slot[-1, -1], 0, 0:1]))

    for r in range(2):
        value = wx[r + 1, 8 : 8 + wide]
        for a in (-1, 0, 1):
            for b in (-1, 0, 1):
                tap = 3 * (a + 1) + (b + 1)
                value = value + taps[tap : tap + 1] * wx[r + 1 - a, 8 - b : 8 - b + wide]
        high = value.astype(BF16).astype(F32)
        low = value - high
        ro[r] = both_low(high, low).astype(BF16)
        ro[r + 2] = both_high(high, low).astype(BF16)
        o1, o2 = split2(jnp.transpose(value))
        for part in range(2):
            rows = slice(part * HD, (part + 1) * HD)
            for place, piece in enumerate((o1, o2, o1, o2)):
                bd[r + 2 * part, place * HD : (place + 1) * HD] = piece[rows]

    sums = []
    for a in (-1, 0, 1):
        for b in (-1, 0, 1):
            total = jnp.sum(
                op[0] * wx[1 - a, 8 - b : 8 - b + wide]
                + op[1] * wx[2 - a, 8 - b : 8 - b + wide],
                0,
                keepdims=True,
            )
            sums.append(total + swap(total))
    first = jnp.concatenate(sums[0:8], 0)
    line = lax.broadcasted_iota(jnp.int32, (8, 128), 0)
    last = jnp.where(line == 0, jnp.broadcast_to(sums[8], (8, 128)), 0.0)
    tap_tile = jnp.where(low_lanes((8, 128)), first, last)

    tzs[...] = tap_tile
    tz_copies = []
    for e, peer in enumerate(z_peers):
        tz_copies.append(send(tzs, tzr.at[z], tz_s.at[e], tz_r.at[e], peer))
    tzr[z] = tap_tile

    def summed(highs, lows, right):
        total = dot(highs[0], right[0]) + dot(lows[0], right[0])
        for r in range(1, ROWS):
            total = total + dot(highs[r], right[r]) + dot(lows[r], right[r])
        total = total + swap(total)
        first = total[0:keys_half]
        total = jnp.where(low_lanes(first.shape), first, total[keys_half : 2 * keys_half])
        return total.reshape(ny, group, pairs, 128)

    def spread(source, target, send_sems, recv_sems):
        copies = []
        for e, peer in enumerate(f_peers):
            a, b = far[e]
            block = source.at[around(y, a, ny), around(g, b, group)]
            copies.append(send(block, target.at[y, g], send_sems.at[e], recv_sems.at[e], peer))
        target[y, g] = source[y, g]
        return copies

    dvb[...] = summed(ph, plo, ro)
    rv_copies = spread(dvb, dvr, rv_s, rv_r)

    query_parts = []
    for r in range(ROWS):
        soft = pf[r]
        prob_grad = dot(av[...], bd[r])
        row_dot = jnp.sum(soft * prob_grad, 0, keepdims=True)
        grad_high, grad_low = split2(soft * (prob_grad - row_dot))
        dh[r] = grad_high
        dlo[r] = grad_low
        both = dot(kt[...], grad_high) + dot(kt[...], grad_low)
        query_parts.append((both[0:HD] + both[HD : 2 * HD]) * (HD ** -0.5))

    dkb[...] = summed(dh, dlo, rq)
    rk_copies = spread(dkb, dkr, rk_s, rk_r)

    for r in range(2):
        dqs[r] = jnp.transpose(jnp.concatenate([query_parts[r], query_parts[r + 2]], 0))
    d_copies = []
    for e, peer in enumerate(x_peers):
        to = pl.multiple_of(around(g, e + 1, group) * COLS, 8)
        source = dqs.at[:, pl.ds(to, COLS), :]
        d_copies.append(send(source, dqr.at[g], d_s.at[e], d_r.at[e], peer))
    dqr[g] = dqs[:, pl.ds(own_q, COLS), :]

    arrive(tz_copies)
    total = tzr[0]
    for i in range(1, nz):
        total = total + tzr[i]
    txs[...] = total
    tx_copies = []
    for e, peer in enumerate(f_peers):
        tx_copies.append(send(txs, txr.at[y, g], tx_s.at[e], tx_r.at[e], peer))
    txr[y, g] = total

    arrive(rv_copies)
    total = dvr[0]
    for i in range(1, ny):
        total = total + dvr[i]
    dvt[...] = total.reshape(group * pairs, 128)
    arrive(rk_copies)
    total = dkr[0]
    for i in range(1, ny):
        total = total + dkr[i]
    dkt[...] = total.reshape(group * pairs, 128)
    for i in range(pairs):
        key_part = dkt[pl.ds(i, group, stride=pairs)]
        value_part = dvt[pl.ds(i, group, stride=pairs)]
        zs[i] = both_low(key_part, value_part)
        zs[i + pairs] = both_high(key_part, value_part)
    rz_copies = []
    for e, peer in enumerate(z_peers):
        to = around(z, z_steps[e], nz)
        rz_copies.append(send(zs.at[to], rsz.at[z], rz_s.at[e], rz_r.at[e], peer))
    rsz[z] = zs[z]

    arrive(d_copies)
    for m in range(group // 2):
        cut = slice(m * 128, (m + 1) * 128)
        for r in range(2):
            dq_ref[r, :, cut] = both_low(dqr[2 * m, r], dqr[2 * m + 1, r])
            dq_ref[r + 2, :, cut] = both_high(dqr[2 * m, r], dqr[2 * m + 1, r])

    arrive(tx_copies)
    tiles = []
    for j in range(group):
        total = txr[0, j]
        for i in range(1, ny):
            total = total + txr[i, j]
        tiles.append(total)
    square = tiles[0] * tiles[0]
    for tile in tiles[1:]:
        square = square + tile * tile
    mean = jnp.sum(square) * (1.0 / (9 * channels))
    scale = jnp.sqrt(jnp.full((8, 128), mean, F32) + 1e-6)
    for m in range(group // 2):
        cut = slice(m * 128, (m + 1) * 128)
        one, two = tiles[2 * m], tiles[2 * m + 1]
        tu_ref[0:8, cut] = both_low(one, two) / scale
        tu_ref[8:9, cut] = (both_high(one, two) / scale)[0:1]

    arrive(rz_copies)
    total = rsz[0]
    for i in range(1, nz):
        total = total + rsz[i]
    for m in range(group // 2):
        cut = slice(m * 128, (m + 1) * 128)
        one, two = total[2 * m : 2 * m + 1], total[2 * m + 1 : 2 * m + 2]
        dk_ref[:, cut] = both_low(one, two)
        dv_ref[:, cut] = both_high(one, two)
    for copy in started:
        copy.wait_send()


def leave(*refs):
    count = len(refs) // 2
    sems = refs[-1]
    copies = []
    for i in range(count):
        copies.append(pltpu.make_async_copy(refs[i], refs[count + i], sems.at[i]))
        copies[i].start()
    for copy in copies:
        copy.wait()


def put_out(results):
    count = len(results)
    return pl.pallas_call(
        leave,
        out_shape=tuple(jax.ShapeDtypeStruct(r.shape, r.dtype) for r in results),
        in_specs=[pl.BlockSpec(memory_space=pltpu.VMEM)] * count,
        out_specs=(pl.BlockSpec(memory_space=pltpu.HBM),) * count,
        scratch_shapes=[pltpu.SemaphoreType.DMA((count,))],
    )(*[pltpu.with_memory_space_constraint(r, pltpu.VMEM) for r in results])


def body(sizes, queries, key_rows, value_rows, cotangent, conv_taps):
    nx, ny, nzl, nzh = sizes
    group = 2 * nx
    nz = nzl * nzh
    wide = group * COLS
    keys = ny * nz * group
    pairs = nz // 2
    channels = group * HD
    vmem = pltpu.VMEM
    scratch = [
        vmem((ROWS, COLS, channels), F32),
        vmem((ROWS, COLS, channels), F32),
        vmem((1, channels), F32),
        vmem((1, channels), F32),
        vmem((9, channels), F32),
        pltpu.SemaphoreType.DMA((5,)),
        vmem((group, 2, COLS, 128), F32),
        vmem((group, 2, COLS, 128), F32),
        vmem((4, wide + 16, 128), F32),
        vmem((2, wide, 128), F32),
        vmem((nz * group, 128), F32),
        vmem((group, pairs, 128), F32),
        vmem((group, pairs, 128), F32),
        vmem((ny, group, pairs, 128), F32),
        vmem((ny, group, pairs, 128), F32),
        vmem((group, COLS // 2, 128), F32),
        vmem((group, COLS // 2, 128), F32),
        vmem((group, COLS // 2, 128), F32),
        vmem((group, COLS // 2, 128), F32),
        vmem((6, 2, 8, 128), F32),
        vmem((16, 128), F32),
        vmem((ROWS, 6 * HD, wide), BF16),
        vmem((ROWS, 4 * HD, wide), BF16),
        vmem((ROWS, wide, 128), BF16),
        vmem((ROWS, wide, 128), BF16),
        vmem((keys, 6 * HD), BF16),
        vmem((keys, 4 * HD), BF16),
        vmem((128, keys), BF16),
        vmem((128, keys), BF16),
        vmem((ROWS, keys, wide), F32),
        vmem((ROWS, keys, wide), BF16),
        vmem((ROWS, keys, wide), BF16),
        vmem((ROWS, keys, wide), BF16),
        vmem((ROWS, keys, wide), BF16),
        vmem((2, wide, 128), F32),
        vmem((2, wide, 128), F32),
        vmem((group, 2, COLS, 128), F32),
        vmem((ny, group, pairs, 128), F32),
        vmem((ny, group, pairs, 128), F32),
        vmem((ny, group, pairs, 128), F32),
        vmem((ny, group, pairs, 128), F32),
        vmem((group * pairs, 128), F32),
        vmem((group * pairs, 128), F32),
        vmem((nz, group, 128), F32),
        vmem((nz, group, 128), F32),
        vmem((8, 128), F32),
        vmem((nz, 8, 128), F32),
        vmem((8, 128), F32),
        vmem((ny, group, 8, 128), F32),
    ]
    plane = ny * group - 1
    counts = (
        group - 1, group - 1, nz - 1, plane, plane, group, group, 6,
        group - 1, plane, plane, nz - 1, nz - 1, plane,
    )
    for count in counts:
        scratch += [pltpu.SemaphoreType.DMA((count,)), pltpu.SemaphoreType.DMA((count,))]
    whole = pl.BlockSpec(memory_space=pltpu.VMEM)
    results = pl.pallas_call(
        functools.partial(kernel, sizes),
        out_shape=(
            jax.ShapeDtypeStruct((ROWS, COLS, channels), F32),
            jax.ShapeDtypeStruct((1, channels), F32),
            jax.ShapeDtypeStruct((1, channels), F32),
            jax.ShapeDtypeStruct((9, channels), F32),
        ),
        in_specs=[pl.BlockSpec(memory_space=pltpu.HBM)] * 5,
        out_specs=(whole,) * 4,
        scratch_shapes=scratch,
        compiler_params=pltpu.CompilerParams(
            collective_id=0, has_side_effects=True, vmem_limit_bytes=48 << 20
        ),
    )(*[pltpu.with_memory_space_constraint(a, pltpu.HBM) for a in (queries, cotangent, key_rows, value_rows, conv_taps)])
    return put_out(results)


def solution(mesh):
    sizes = (NX, NY, mesh.shape["lon"] // (2 * NX), mesh.shape["lat"] // NY)
    placed = (
        P("lat", "lon", None),
        P(("lat", "lon"), None),
        P(("lat", "lon"), None),
        P("lat", "lon", None),
        P(),
    )
    return jax.shard_map(
        functools.partial(body, sizes),
        mesh=mesh,
        in_specs=placed,
        out_specs=(P("lat", "lon", None), P(("lat", "lon"), None), P(("lat", "lon"), None), P()),
        check_vma=False,
    )
```

```python
import functools

import jax
import jax.numpy as jnp
import numpy as np
from jax import lax
from jax.experimental import pallas as pl
from jax.experimental.pallas import tpu as pltpu
from jax.sharding import PartitionSpec as P

HD = 64
NX = 4
NY = 4
ROWS = 4
COLS = 32
F32 = jnp.float32
BF16 = jnp.bfloat16
MESH = pl.DeviceIdType.MESH


def low_lanes(shape):
    return lax.broadcasted_iota(jnp.int32, shape, len(shape) - 1) < HD


def swap(value):
    return pltpu.roll(value, HD, value.ndim - 1)


def both_low(first, second):
    return jnp.where(low_lanes(first.shape), first, swap(second))


def both_high(first, second):
    return jnp.where(low_lanes(first.shape), swap(first), second)


def split2(value):
    high = value.astype(BF16)
    return high, (value - high.astype(F32)).astype(BF16)


def split3(value):
    first = value.astype(BF16)
    rest = value - first.astype(F32)
    second = rest.astype(BF16)
    return first, second, (rest - second.astype(F32)).astype(BF16)


def dot(a, b):
    return jnp.dot(a, b, preferred_element_type=F32)


def kernel(
    sizes,
    q_hbm, c_hbm, k_hbm, v_hbm, t_hbm,
    dq_ref, dk_ref, dv_ref, tu_ref,
    q_ref, c_ref, k_ref, v_ref, t_ref, in_s,
    ws, qs, wx, qx, kvz, ks, vs, kp, vp, hus, hds, hu, hd, hb,
    taps, bs, bd, rq, ro, ak, av, kt, vt, pf, ph, plo, dh, dlo, op, dqs, dqr,
    dvb, dkb, dvr, dkr, dvt, dkt, zs, rsz, tzs, tzr, txs, txr,
    w_s, w_r, q_s, q_r, z_s, z_r, k_s, k_r, v_s, v_r, u_s, u_r, n_s, n_r, h_s, h_r,
    d_s, d_r, rv_s, rv_r, rk_s, rk_r, rz_s, rz_r, tz_s, tz_r, tx_s, tx_r, met,
):
    nx, ny, nzl, nzh = sizes
    group = 2 * nx
    nz = nzl * nzh
    band_count = nzh * ny
    wide = group * COLS
    pairs = nz // 2
    keys_half = ny * group * pairs
    channels = group * HD
    lat = lax.axis_index("lat")
    lon = lax.axis_index("lon")
    y = lax.rem(lat, ny)
    z_hi = lax.div(lat, ny)
    z_lo = lax.div(lon, group)
    g = lax.rem(lon, group)
    z = z_hi * nzl + z_lo
    here = y * group + g
    plane = ny * group - 1

    def at(z_of, y_of, g_of):
        return (lax.div(z_of, nzl) * ny + y_of, lax.rem(z_of, nzl) * group + g_of)

    def around(value, step, count):
        return lax.rem(value + step + count, count)

    x_peers = [at(z, y, around(g, e, group)) for e in range(1, group)]
    z_steps = sorted(range(1, nz), key=lambda e: -min(e, nz - e))
    z_peers = [at(around(z, e, nz), y, g) for e in z_steps]
    far = [(a, b) for a in range(ny) for b in range(group) if a or b]
    far = sorted(far, key=lambda s: -min(s[0], ny - s[0]) - min(s[1], group - s[1]) / 2)
    f_peers = [at(z, around(y, a, ny), around(g, b, group)) for a, b in far]

    def beside(d_lat, d_lon, to):
        return (around(lat, d_lat, band_count), around(z_lo, d_lon, nzl) * group + to)

    u_peers = [beside(1, 0, around(g, e, group)) for e in range(group)]
    n_peers = [beside(-1, 0, around(g, e, group)) for e in range(group)]
    h_steps = [(a, b) for a in (-1, 0, 1) for b in (1, -1)]
    h_peers = [beside(a, b, g) for a, b in h_steps]

    barrier = pltpu.get_barrier_semaphore()
    inputs = []
    for i, (source, target) in enumerate(
        ((k_hbm, k_ref), (v_hbm, v_ref), (c_hbm, c_ref), (q_hbm, q_ref), (t_hbm, t_ref))
    ):
        inputs.append(pltpu.make_async_copy(source, target, in_s.at[i]))
        inputs[i].start()
    y_peers = [at(z, around(y, e, ny), g) for e in range(1, ny)]
    bands = [beside(1, 0, g), beside(-1, 0, g)]
    sides = [beside(0, 1, g), beside(0, -1, g)]
    partners = z_peers + bands + y_peers + x_peers
    for peer in partners:
        pl.semaphore_signal(barrier, inc=1, device_id=peer, device_id_type=MESH)

    def send(source, target, send_sem, recv_sem, peer):
        copy = pltpu.make_async_remote_copy(
            src_ref=source, dst_ref=target, send_sem=send_sem, recv_sem=recv_sem,
            device_id=peer, device_id_type=MESH,
        )
        copy.start()

    started = []
    arrived = []

    def phase(block, send_sem, recv_sem):
        copies = pltpu.make_async_remote_copy(
            src_ref=block, dst_ref=block, send_sem=send_sem, recv_sem=recv_sem,
            device_id=x_peers[0], device_id_type=MESH,
        )
        started.append(copies)
        return copies

    def arrive(*phases):
        for copies in phases:
            copies.wait_recv()
            arrived.append(copies)

    inputs[0].wait()
    inputs[1].wait()
    rows = []
    for m in range(group // 2):
        cut = slice(m * 128, (m + 1) * 128)
        rows.append(both_low(k_ref[:, cut], v_ref[:, cut]))
        rows.append(both_high(k_ref[:, cut], v_ref[:, cut]))
    own_z = pl.ds(pl.multiple_of(z * group, group), group)
    kvz[own_z] = jnp.concatenate(rows, 0)
    own_w = pl.multiple_of(8 + COLS * g, 8)
    own_q = pl.multiple_of(COLS * g, 8)

    pl.semaphore_wait(barrier, len(partners))

    z_copies = phase(kvz.at[pl.ds(0, (nz - 1) * group)], z_s, z_r)
    for e, peer in enumerate(z_peers):
        send(kvz.at[own_z], kvz.at[own_z], z_s, z_r, peer)
    relays = bands + y_peers + sides
    for peer in relays:
        pl.semaphore_signal(met, inc=1, device_id=peer, device_id_type=MESH)

    inputs[2].wait()
    line_total = ROWS * band_count
    centres = (np.arange(line_total) + 0.5) * np.pi / line_total
    mean_cosine = float(np.mean(np.sin(centres)))
    line = lax.broadcasted_iota(jnp.int32, (8, 128), 0) + lat * ROWS
    weight = jnp.sin((line.astype(F32) + 0.5) * (np.pi / line_total)) / mean_cosine
    for m in range(group // 2):
        cut = slice(m * 128, (m + 1) * 128)
        for r in range(2):
            upper = c_ref[r, :, cut] * weight[r : r + 1]
            lower = c_ref[r + 2, :, cut] * weight[r + 2 : r + 3]
            ws[2 * m, r] = both_low(upper, lower)
            ws[2 * m + 1, r] = both_high(upper, lower)
            if r == 0:
                hds[2 * m] = both_low(upper[: COLS // 2], upper[COLS // 2 :])
                hds[2 * m + 1] = both_high(upper[: COLS // 2], upper[COLS // 2 :])
            else:
                hus[2 * m] = both_low(lower[: COLS // 2], lower[COLS // 2 :])
                hus[2 * m + 1] = both_high(lower[: COLS // 2], lower[COLS // 2 :])
    w_copies = phase(ws.at[pl.ds(0, group - 1)], w_s, w_r)
    for e, peer in enumerate(x_peers):
        to = around(g, e + 1, group)
        target = wx.at[pl.ds(1, 2), pl.ds(own_w, COLS), :]
        send(ws.at[to], target, w_s, w_r, peer)
    wx[pl.ds(1, 2), pl.ds(own_w, COLS), :] = ws[g]
    inputs[3].wait()
    for m in range(group // 2):
        cut = slice(m * 128, (m + 1) * 128)
        for r in range(2):
            upper = q_ref[r, :, cut] * (HD ** -0.5)
            lower = q_ref[r + 2, :, cut] * (HD ** -0.5)
            qs[2 * m, r] = both_low(upper, lower)
            qs[2 * m + 1, r] = both_high(upper, lower)
    q_copies = phase(qs.at[pl.ds(0, group - 1)], q_s, q_r)
    for e, peer in enumerate(x_peers):
        to = around(g, e + 1, group)
        target = qx.at[:, pl.ds(own_q, COLS), :]
        send(qs.at[to], target, q_s, q_r, peer)
    qx[:, pl.ds(own_q, COLS), :] = qs[g]
    pl.semaphore_wait(met, len(relays))
    u_copies = phase(hu, u_s, u_r)
    n_copies = phase(hd, n_s, n_r)
    for e in range(group):
        to = around(g, e, group)
        send(hus.at[to], hu.at[g], u_s, u_r, u_peers[e])
        send(hds.at[to], hd.at[g], n_s, n_r, n_peers[e])

    arrive(z_copies)
    for h in range(group):
        first = kvz[pl.ds(h, pairs, stride=group)]
        second = kvz[pl.ds(h + group * pairs, pairs, stride=group)]
        ks[h] = both_low(first, second)
        vs[h] = both_high(first, second)
    k_copies = phase(kp.at[pl.ds(0, plane)], k_s, k_r)
    for e, peer in enumerate(f_peers):
        to = around(g, far[e][1], group)
        send(ks.at[to], kp.at[here], k_s, k_r, peer)
    v_copies = phase(vp.at[pl.ds(0, plane)], v_s, v_r)
    for e, peer in enumerate(f_peers):
        to = around(g, far[e][1], group)
        send(vs.at[to], vp.at[here], v_s, v_r, peer)
    kp[here] = ks[g]
    vp[here] = vs[g]

    arrive(w_copies)
    h_copies = phase(hb, h_s, h_r)
    for i, (a, b) in enumerate(h_steps):
        source = wx.at[pl.ds(1, 2), pl.ds(wide if b == 1 else 8, 8), :]
        send(source, hb.at[i], h_s, h_r, h_peers[i])

    arrive(q_copies)
    for r in range(2):
        value = qx[r]
        high = value.astype(BF16).astype(F32)
        low = value - high
        rq[r] = both_low(high, low).astype(BF16)
        rq[r + 2] = both_high(high, low).astype(BF16)
        q1, q2, q3 = split3(jnp.transpose(value))
        for part in range(2):
            rows = slice(part * HD, (part + 1) * HD)
            for place, piece in enumerate((q1, q2, q1, q2, q3, q1)):
                bs[r + 2 * part, place * HD : (place + 1) * HD] = piece[rows]

    pair = pl.multiple_of(lax.div(g, 2) * 128, 128)
    inputs[4].wait()
    taps[0:9] = t_ref[:, pl.ds(pair, 128)]
    taken = taps[...]
    low = low_lanes(taken.shape)
    even = jnp.where(low, taken, swap(taken))
    odd = jnp.where(low, swap(taken), taken)
    taps[...] = jnp.where(lax.rem(g, 2) == 0, even, odd)

    def wide_pieces(value):
        s1 = value.astype(BF16).astype(F32)
        rest = value - s1
        s2 = rest.astype(BF16).astype(F32)
        s3 = rest - s2
        low = low_lanes(value.shape)

        def both(a, b):
            first = jnp.where(low, a, swap(b)).astype(BF16)
            return first, jnp.where(low, swap(a), b).astype(BF16)

        return both(s1, s1), both(s2, s2), both(s1, s3)

    def turned_pieces(value, target):
        for i, piece in enumerate(split2(jnp.transpose(value))):
            target[i * HD : (i + 1) * HD, 0:keys_half] = piece[0:HD]
            target[i * HD : (i + 1) * HD, keys_half : 2 * keys_half] = piece[HD : 2 * HD]

    arrive(k_copies)
    value = kp[...].reshape(keys_half, 128)
    for i, (first, second) in enumerate(wide_pieces(value)):
        ak[0:keys_half, i * 128 : (i + 1) * 128] = first
        ak[keys_half : 2 * keys_half, i * 128 : (i + 1) * 128] = second
    turned_pieces(value, kt)

    out_parts = []
    for r in range(ROWS):
        logits = dot(ak[...], bs[r])
        raised = jnp.exp(logits - jnp.max(logits, 0, keepdims=True))
        soft = raised * (1.0 / jnp.sum(raised, 0, keepdims=True))
        soft_high, soft_low = split2(soft)
        pf[r] = soft
        ph[r] = soft_high
        plo[r] = soft_low

    arrive(v_copies)
    value = vp[...].reshape(keys_half, 128)
    for i, (first, second) in enumerate(wide_pieces(value)[0:2]):
        av[0:keys_half, i * 128 : (i + 1) * 128] = first
        av[keys_half : 2 * keys_half, i * 128 : (i + 1) * 128] = second
    turned_pieces(value, vt)
    for r in range(ROWS):
        both = dot(vt[...], ph[r]) + dot(vt[...], plo[r])
        out_parts.append(both[0:HD] + both[HD : 2 * HD])
    for r in range(2):
        op[r] = jnp.transpose(jnp.concatenate([out_parts[r], out_parts[r + 2]], 0))

    arrive(h_copies, u_copies, n_copies)
    slot = {step: i for i, step in enumerate(h_steps)}
    left, right = 7, 8 + wide
    for r in range(2):
        wx[r + 1, left : left + 1] = hb[slot[0, 1], r, 7:8]
        wx[r + 1, right : right + 1] = hb[slot[0, -1], r, 0:1]
    top = jnp.where(lat > 0, 1.0, 0.0)
    bottom = jnp.where(lat < band_count - 1, 1.0, 0.0)

    def above(low_part, own):
        return jnp.where(low_lanes(own.shape), low_part * top, swap(own))

    def below(own, high_part):
        return jnp.where(low_lanes(own.shape), swap(own), high_part * bottom)

    part = COLS // 2
    for j in range(group):
        one = slice(8 + COLS * j, 8 + COLS * j + part)
        two = slice(8 + COLS * j + part, 8 + COLS * (j + 1))
        wx[0, one] = above(hu[j], wx[2, one])
        wx[0, two] = above(swap(hu[j]), wx[2, two])
        wx[3, one] = below(wx[1, one], swap(hd[j]))
        wx[3, two] = below(wx[1, two], hd[j])
    wx[0, left : left + 1] = above(swap(hb[slot[1, 1], 1, 7:8]), wx[2, left : left + 1])
    wx[0, right : right + 1] = above(swap(hb[slot[1, -1], 1, 0:1]), wx[2, right : right + 1])
    wx[3, left : left + 1] = below(wx[1, left : left + 1], swap(hb[slot[-1, 1], 0, 7:8]))
    wx[3, right : right + 1] = below(wx[1, right : right + 1], swap(hb[slot[-1, -1], 0, 0:1]))

    for r in range(2):
        value = wx[r + 1, 8 : 8 + wide]
        for a in (-1, 0, 1):
            for b in (-1, 0, 1):
                tap = 3 * (a + 1) + (b + 1)
                value = value + taps[tap : tap + 1] * wx[r + 1 - a, 8 - b : 8 - b + wide]
        high = value.astype(BF16).astype(F32)
        low = value - high
        ro[r] = both_low(high, low).astype(BF16)
        ro[r + 2] = both_high(high, low).astype(BF16)
        o1, o2 = split2(jnp.transpose(value))
        for part in range(2):
            rows = slice(part * HD, (part + 1) * HD)
            for place, piece in enumerate((o1, o2, o1, o2)):
                bd[r + 2 * part, place * HD : (place + 1) * HD] = piece[rows]

    sums = []
    for a in (-1, 0, 1):
        for b in (-1, 0, 1):
            total = jnp.sum(
                op[0] * wx[1 - a, 8 - b : 8 - b + wide]
                + op[1] * wx[2 - a, 8 - b : 8 - b + wide],
                0,
                keepdims=True,
            )
            sums.append(total + swap(total))
    first = jnp.concatenate(sums[0:8], 0)
    line = lax.broadcasted_iota(jnp.int32, (8, 128), 0)
    last = jnp.where(line == 0, jnp.broadcast_to(sums[8], (8, 128)), 0.0)
    tap_tile = jnp.where(low_lanes((8, 128)), first, last)

    tzs[...] = tap_tile
    tz_copies = phase(tzr.at[pl.ds(0, nz - 1)], tz_s, tz_r)
    for e, peer in enumerate(z_peers):
        send(tzs, tzr.at[z], tz_s, tz_r, peer)
    tzr[z] = tap_tile

    def summed(highs, lows, right):
        total = dot(highs[0], right[0]) + dot(lows[0], right[0])
        for r in range(1, ROWS):
            total = total + dot(highs[r], right[r]) + dot(lows[r], right[r])
        total = total + swap(total)
        first = total[0:keys_half]
        total = jnp.where(low_lanes(first.shape), first, total[keys_half : 2 * keys_half])
        return total.reshape(ny * group, pairs, 128)

    def spread(source, target, send_sem, recv_sem):
        copies = phase(target.at[pl.ds(0, plane)], send_sem, recv_sem)
        for e, peer in enumerate(f_peers):
            a, b = far[e]
            block = source.at[around(y, a, ny) * group + around(g, b, group)]
            send(block, target.at[here], send_sem, recv_sem, peer)
        target[here] = source[here]
        return copies

    dvb[...] = summed(ph, plo, ro)
    rv_copies = spread(dvb, dvr, rv_s, rv_r)

    query_parts = []
    for r in range(ROWS):
        soft = pf[r]
        prob_grad = dot(av[...], bd[r])
        row_dot = jnp.sum(soft * prob_grad, 0, keepdims=True)
        grad_high, grad_low = split2(soft * (prob_grad - row_dot))
        dh[r] = grad_high
        dlo[r] = grad_low
        both = dot(kt[...], grad_high) + dot(kt[...], grad_low)
        query_parts.append((both[0:HD] + both[HD : 2 * HD]) * (HD ** -0.5))

    dkb[...] = summed(dh, dlo, rq)
    rk_copies = spread(dkb, dkr, rk_s, rk_r)

    for r in range(2):
        dqs[r] = jnp.transpose(jnp.concatenate([query_parts[r], query_parts[r + 2]], 0))
    d_copies = phase(dqr.at[pl.ds(0, group - 1)], d_s, d_r)
    for e, peer in enumerate(x_peers):
        to = pl.multiple_of(around(g, e + 1, group) * COLS, 8)
        source = dqs.at[:, pl.ds(to, COLS), :]
        send(source, dqr.at[g], d_s, d_r, peer)
    dqr[g] = dqs[:, pl.ds(own_q, COLS), :]

    arrive(tz_copies)
    total = tzr[0]
    for i in range(1, nz):
        total = total + tzr[i]
    txs[...] = total
    tx_copies = phase(txr.at[pl.ds(0, plane)], tx_s, tx_r)
    for e, peer in enumerate(f_peers):
        send(txs, txr.at[here], tx_s, tx_r, peer)
    txr[here] = total

    arrive(rv_copies)
    total = dvr[0:group]
    for i in range(1, ny):
        total = total + dvr[i * group : (i + 1) * group]
    dvt[...] = total.reshape(group * pairs, 128)
    arrive(rk_copies)
    total = dkr[0:group]
    for i in range(1, ny):
        total = total + dkr[i * group : (i + 1) * group]
    dkt[...] = total.reshape(group * pairs, 128)
    for i in range(pairs):
        key_part = dkt[pl.ds(i, group, stride=pairs)]
        value_part = dvt[pl.ds(i, group, stride=pairs)]
        zs[i] = both_low(key_part, value_part)
        zs[i + pairs] = both_high(key_part, value_part)
    rz_copies = phase(rsz.at[pl.ds(0, nz - 1)], rz_s, rz_r)
    for e, peer in enumerate(z_peers):
        to = around(z, z_steps[e], nz)
        send(zs.at[to], rsz.at[z], rz_s, rz_r, peer)
    rsz[z] = zs[z]

    arrive(d_copies)
    for m in range(group // 2):
        cut = slice(m * 128, (m + 1) * 128)
        for r in range(2):
            dq_ref[r, :, cut] = both_low(dqr[2 * m, r], dqr[2 * m + 1, r])
            dq_ref[r + 2, :, cut] = both_high(dqr[2 * m, r], dqr[2 * m + 1, r])

    arrive(tx_copies)
    tiles = []
    for j in range(group):
        total = txr[j]
        for i in range(1, ny):
            total = total + txr[i * group + j]
        tiles.append(total)
    square = tiles[0] * tiles[0]
    for tile in tiles[1:]:
        square = square + tile * tile
    mean = jnp.sum(square) * (1.0 / (9 * channels))
    scale = jnp.sqrt(jnp.full((8, 128), mean, F32) + 1e-6)
    for m in range(group // 2):
        cut = slice(m * 128, (m + 1) * 128)
        one, two = tiles[2 * m], tiles[2 * m + 1]
        tu_ref[0:8, cut] = both_low(one, two) / scale
        tu_ref[8:9, cut] = (both_high(one, two) / scale)[0:1]

    arrive(rz_copies)
    total = rsz[0]
    for i in range(1, nz):
        total = total + rsz[i]
    for m in range(group // 2):
        cut = slice(m * 128, (m + 1) * 128)
        one, two = total[2 * m : 2 * m + 1], total[2 * m + 1 : 2 * m + 2]
        dk_ref[:, cut] = both_low(one, two)
        dv_ref[:, cut] = both_high(one, two)
    for copy in started:
        copy.wait_send()


def leave(*refs):
    count = len(refs) // 2
    sems = refs[-1]
    copies = []
    for i in range(count):
        copies.append(pltpu.make_async_copy(refs[i], refs[count + i], sems.at[i]))
        copies[i].start()
    for copy in copies:
        copy.wait()


def put_out(results):
    count = len(results)
    return pl.pallas_call(
        leave,
        out_shape=tuple(jax.ShapeDtypeStruct(r.shape, r.dtype) for r in results),
        in_specs=[pl.BlockSpec(memory_space=pltpu.VMEM)] * count,
        out_specs=(pl.BlockSpec(memory_space=pltpu.HBM),) * count,
        scratch_shapes=[pltpu.SemaphoreType.DMA((count,))],
    )(*[pltpu.with_memory_space_constraint(r, pltpu.VMEM) for r in results])


def body(sizes, queries, key_rows, value_rows, cotangent, conv_taps):
    nx, ny, nzl, nzh = sizes
    group = 2 * nx
    nz = nzl * nzh
    wide = group * COLS
    keys = ny * nz * group
    pairs = nz // 2
    channels = group * HD
    vmem = pltpu.VMEM
    scratch = [
        vmem((ROWS, COLS, channels), F32),
        vmem((ROWS, COLS, channels), F32),
        vmem((1, channels), F32),
        vmem((1, channels), F32),
        vmem((9, channels), F32),
        pltpu.SemaphoreType.DMA((5,)),
        vmem((group, 2, COLS, 128), F32),
        vmem((group, 2, COLS, 128), F32),
        vmem((4, wide + 16, 128), F32),
        vmem((2, wide, 128), F32),
        vmem((nz * group, 128), F32),
        vmem((group, pairs, 128), F32),
        vmem((group, pairs, 128), F32),
        vmem((ny * group, pairs, 128), F32),
        vmem((ny * group, pairs, 128), F32),
        vmem((group, COLS // 2, 128), F32),
        vmem((group, COLS // 2, 128), F32),
        vmem((group, COLS // 2, 128), F32),
        vmem((group, COLS // 2, 128), F32),
        vmem((6, 2, 8, 128), F32),
        vmem((16, 128), F32),
        vmem((ROWS, 6 * HD, wide), BF16),
        vmem((ROWS, 4 * HD, wide), BF16),
        vmem((ROWS, wide, 128), BF16),
        vmem((ROWS, wide, 128), BF16),
        vmem((keys, 6 * HD), BF16),
        vmem((keys, 4 * HD), BF16),
        vmem((128, keys), BF16),
        vmem((128, keys), BF16),
        vmem((ROWS, keys, wide), F32),
        vmem((ROWS, keys, wide), BF16),
        vmem((ROWS, keys, wide), BF16),
        vmem((ROWS, keys, wide), BF16),
        vmem((ROWS, keys, wide), BF16),
        vmem((2, wide, 128), F32),
        vmem((2, wide, 128), F32),
        vmem((group, 2, COLS, 128), F32),
        vmem((ny * group, pairs, 128), F32),
        vmem((ny * group, pairs, 128), F32),
        vmem((ny * group, pairs, 128), F32),
        vmem((ny * group, pairs, 128), F32),
        vmem((group * pairs, 128), F32),
        vmem((group * pairs, 128), F32),
        vmem((nz, group, 128), F32),
        vmem((nz, group, 128), F32),
        vmem((8, 128), F32),
        vmem((nz, 8, 128), F32),
        vmem((8, 128), F32),
        vmem((ny * group, 8, 128), F32),
    ]
    scratch += [pltpu.SemaphoreType.DMA] * 28
    scratch.append(pltpu.SemaphoreType.REGULAR)
    whole = pl.BlockSpec(memory_space=pltpu.VMEM)
    results = pl.pallas_call(
        functools.partial(kernel, sizes),
        out_shape=(
            jax.ShapeDtypeStruct((ROWS, COLS, channels), F32),
            jax.ShapeDtypeStruct((1, channels), F32),
            jax.ShapeDtypeStruct((1, channels), F32),
            jax.ShapeDtypeStruct((9, channels), F32),
        ),
        in_specs=[pl.BlockSpec(memory_space=pltpu.HBM)] * 5,
        out_specs=(whole,) * 4,
        scratch_shapes=scratch,
        compiler_params=pltpu.CompilerParams(
            collective_id=0, has_side_effects=True, vmem_limit_bytes=48 << 20
        ),
    )(*[pltpu.with_memory_space_constraint(a, pltpu.HBM) for a in (queries, cotangent, key_rows, value_rows, conv_taps)])
    return put_out(results)


def solution(mesh):
    sizes = (NX, NY, mesh.shape["lon"] // (2 * NX), mesh.shape["lat"] // NY)
    placed = (
        P("lat", "lon", None),
        P(("lat", "lon"), None),
        P(("lat", "lon"), None),
        P("lat", "lon", None),
        P(),
    )
    return jax.shard_map(
        functools.partial(body, sizes),
        mesh=mesh,
        in_specs=placed,
        out_specs=(P("lat", "lon", None), P(("lat", "lon"), None), P(("lat", "lon"), None), P()),
        check_vma=False,
    )
```

```python
import functools

import jax
import jax.numpy as jnp
import numpy as np
from jax import lax
from jax.experimental import pallas as pl
from jax.experimental.pallas import tpu as pltpu
from jax.sharding import PartitionSpec as P

HD = 64
NX = 4
NY = 4
ROWS = 4
COLS = 32
F32 = jnp.float32
BF16 = jnp.bfloat16
MESH = pl.DeviceIdType.MESH


def low_lanes(shape):
    return lax.broadcasted_iota(jnp.int32, shape, len(shape) - 1) < HD


def swap(value):
    return pltpu.roll(value, HD, value.ndim - 1)


def both_low(first, second):
    return jnp.where(low_lanes(first.shape), first, swap(second))


def both_high(first, second):
    return jnp.where(low_lanes(first.shape), swap(first), second)


def split2(value):
    high = value.astype(BF16)
    return high, (value - high.astype(F32)).astype(BF16)


def split3(value):
    first = value.astype(BF16)
    rest = value - first.astype(F32)
    second = rest.astype(BF16)
    return first, second, (rest - second.astype(F32)).astype(BF16)


def dot(a, b):
    return jnp.dot(a, b, preferred_element_type=F32)


def kernel(
    sizes,
    q_hbm, c_hbm, k_hbm, v_hbm, t_hbm,
    dq_ref, dk_ref, dv_ref, tu_ref,
    q_ref, c_ref, k_ref, v_ref, t_ref, in_s,
    ws, qs, wx, qx, kvz, ks, vs, kp, vp, hus, hds, hu, hd, hb,
    taps, bs, bd, rq, ro, ak, av, kt, vt, pf, ph, plo, dh, dlo, op, dqs, dqr,
    dvb, dkb, dvr, dkr, dvt, dkt, zs, rsz, tzs, tzr, txs, txr,
    w_s, w_r, q_s, q_r, z_s, z_r, k_s, k_r, v_s, v_r, u_s, u_r, n_s, n_r, h_s, h_r,
    d_s, d_r, rv_s, rv_r, rk_s, rk_r, rz_s, rz_r, tz_s, tz_r, tx_s, tx_r, met,
):
    nx, ny, nzl, nzh = sizes
    group = 2 * nx
    nz = nzl * nzh
    band_count = nzh * ny
    wide = group * COLS
    pairs = nz // 2
    keys_half = ny * group * pairs
    channels = group * HD
    lat = lax.axis_index("lat")
    lon = lax.axis_index("lon")
    y = lax.rem(lat, ny)
    z_hi = lax.div(lat, ny)
    z_lo = lax.div(lon, group)
    g = lax.rem(lon, group)
    z = z_hi * nzl + z_lo
    here = y * group + g
    plane = ny * group - 1

    def at(z_of, y_of, g_of):
        return (lax.div(z_of, nzl) * ny + y_of, lax.rem(z_of, nzl) * group + g_of)

    def around(value, step, count):
        return lax.rem(value + step + count, count)

    x_peers = [at(z, y, around(g, e, group)) for e in range(1, group)]
    z_steps = sorted(range(1, nz), key=lambda e: -min(e, nz - e))
    z_peers = [at(around(z, e, nz), y, g) for e in z_steps]
    far = [(a, b) for a in range(ny) for b in range(group) if a or b]
    far = sorted(far, key=lambda s: min(s[0], ny - s[0]) + min(s[1], group - s[1]) / 2)
    f_peers = [at(z, around(y, a, ny), around(g, b, group)) for a, b in far]

    def beside(d_lat, d_lon, to):
        return (around(lat, d_lat, band_count), around(z_lo, d_lon, nzl) * group + to)

    u_peers = [beside(1, 0, around(g, e, group)) for e in range(group)]
    n_peers = [beside(-1, 0, around(g, e, group)) for e in range(group)]
    h_steps = [(a, b) for a in (-1, 0, 1) for b in (1, -1)]
    h_peers = [beside(a, b, g) for a, b in h_steps]

    barrier = pltpu.get_barrier_semaphore()
    inputs = []
    for i, (source, target) in enumerate(
        ((k_hbm, k_ref), (v_hbm, v_ref), (c_hbm, c_ref), (q_hbm, q_ref), (t_hbm, t_ref))
    ):
        inputs.append(pltpu.make_async_copy(source, target, in_s.at[i]))
        inputs[i].start()
    y_peers = [at(z, around(y, e, ny), g) for e in range(1, ny)]
    bands = [beside(1, 0, g), beside(-1, 0, g)]
    sides = [beside(0, 1, g), beside(0, -1, g)]
    partners = z_peers + bands + y_peers + x_peers
    for peer in partners:
        pl.semaphore_signal(barrier, inc=1, device_id=peer, device_id_type=MESH)

    def send(source, target, send_sem, recv_sem, peer):
        copy = pltpu.make_async_remote_copy(
            src_ref=source, dst_ref=target, send_sem=send_sem, recv_sem=recv_sem,
            device_id=peer, device_id_type=MESH,
        )
        copy.start()

    started = []
    arrived = []

    def phase(block, send_sem, recv_sem):
        copies = pltpu.make_async_remote_copy(
            src_ref=block, dst_ref=block, send_sem=send_sem, recv_sem=recv_sem,
            device_id=x_peers[0], device_id_type=MESH,
        )
        started.append(copies)
        return copies

    def arrive(*phases):
        for copies in phases:
            copies.wait_recv()
            arrived.append(copies)

    inputs[0].wait()
    inputs[1].wait()
    rows = []
    for m in range(group // 2):
        cut = slice(m * 128, (m + 1) * 128)
        rows.append(both_low(k_ref[:, cut], v_ref[:, cut]))
        rows.append(both_high(k_ref[:, cut], v_ref[:, cut]))
    own_z = pl.ds(pl.multiple_of(z * group, group), group)
    kvz[own_z] = jnp.concatenate(rows, 0)
    own_w = pl.multiple_of(8 + COLS * g, 8)
    own_q = pl.multiple_of(COLS * g, 8)

    pl.semaphore_wait(barrier, len(partners))

    z_copies = phase(kvz.at[pl.ds(0, (nz - 1) * group)], z_s, z_r)
    for e, peer in enumerate(z_peers):
        send(kvz.at[own_z], kvz.at[own_z], z_s, z_r, peer)
    relays = bands + y_peers + sides
    for peer in relays:
        pl.semaphore_signal(met, inc=1, device_id=peer, device_id_type=MESH)

    inputs[2].wait()
    line_total = ROWS * band_count
    centres = (np.arange(line_total) + 0.5) * np.pi / line_total
    mean_cosine = float(np.mean(np.sin(centres)))
    line = lax.broadcasted_iota(jnp.int32, (8, 128), 0) + lat * ROWS
    weight = jnp.sin((line.astype(F32) + 0.5) * (np.pi / line_total)) / mean_cosine
    for m in range(group // 2):
        cut = slice(m * 128, (m + 1) * 128)
        for r in range(2):
            upper = c_ref[r, :, cut] * weight[r : r + 1]
            lower = c_ref[r + 2, :, cut] * weight[r + 2 : r + 3]
            ws[2 * m, r] = both_low(upper, lower)
            ws[2 * m + 1, r] = both_high(upper, lower)
            if r == 0:
                hds[2 * m] = both_low(upper[: COLS // 2], upper[COLS // 2 :])
                hds[2 * m + 1] = both_high(upper[: COLS // 2], upper[COLS // 2 :])
            else:
                hus[2 * m] = both_low(lower[: COLS // 2], lower[COLS // 2 :])
                hus[2 * m + 1] = both_high(lower[: COLS // 2], lower[COLS // 2 :])
    w_copies = phase(ws.at[pl.ds(0, group - 1)], w_s, w_r)
    for e, peer in enumerate(x_peers):
        to = around(g, e + 1, group)
        target = wx.at[pl.ds(1, 2), pl.ds(own_w, COLS), :]
        send(ws.at[to], target, w_s, w_r, peer)
    wx[pl.ds(1, 2), pl.ds(own_w, COLS), :] = ws[g]
    inputs[3].wait()
    for m in range(group // 2):
        cut = slice(m * 128, (m + 1) * 128)
        for r in range(2):
            upper = q_ref[r, :, cut] * (HD ** -0.5)
            lower = q_ref[r + 2, :, cut] * (HD ** -0.5)
            qs[2 * m, r] = both_low(upper, lower)
            qs[2 * m + 1, r] = both_high(upper, lower)
    q_copies = phase(qs.at[pl.ds(0, group - 1)], q_s, q_r)
    for e, peer in enumerate(x_peers):
        to = around(g, e + 1, group)
        target = qx.at[:, pl.ds(own_q, COLS), :]
        send(qs.at[to], target, q_s, q_r, peer)
    qx[:, pl.ds(own_q, COLS), :] = qs[g]
    pl.semaphore_wait(met, len(relays))
    u_copies = phase(hu, u_s, u_r)
    n_copies = phase(hd, n_s, n_r)
    for e in range(group):
        to = around(g, e, group)
        send(hus.at[to], hu.at[g], u_s, u_r, u_peers[e])
        send(hds.at[to], hd.at[g], n_s, n_r, n_peers[e])

    arrive(z_copies)
    for h in range(group):
        first = kvz[pl.ds(h, pairs, stride=group)]
        second = kvz[pl.ds(h + group * pairs, pairs, stride=group)]
        ks[h] = both_low(first, second)
        vs[h] = both_high(first, second)
    k_copies = phase(kp.at[pl.ds(0, plane)], k_s, k_r)
    for e, peer in enumerate(f_peers):
        to = around(g, far[e][1], group)
        send(ks.at[to], kp.at[here], k_s, k_r, peer)
    v_copies = phase(vp.at[pl.ds(0, plane)], v_s, v_r)
    for e, peer in enumerate(f_peers):
        to = around(g, far[e][1], group)
        send(vs.at[to], vp.at[here], v_s, v_r, peer)
    kp[here] = ks[g]
    vp[here] = vs[g]

    arrive(w_copies)
    h_copies = phase(hb, h_s, h_r)
    for i, (a, b) in enumerate(h_steps):
        source = wx.at[pl.ds(1, 2), pl.ds(wide if b == 1 else 8, 8), :]
        send(source, hb.at[i], h_s, h_r, h_peers[i])

    arrive(q_copies)
    for r in range(2):
        value = qx[r]
        high = value.astype(BF16).astype(F32)
        low = value - high
        rq[r] = both_low(high, low).astype(BF16)
        rq[r + 2] = both_high(high, low).astype(BF16)
        q1, q2, q3 = split3(jnp.transpose(value))
        for part in range(2):
            rows = slice(part * HD, (part + 1) * HD)
            for place, piece in enumerate((q1, q2, q1, q2, q3, q1)):
                bs[r + 2 * part, place * HD : (place + 1) * HD] = piece[rows]

    pair = pl.multiple_of(lax.div(g, 2) * 128, 128)
    inputs[4].wait()
    taps[0:9] = t_ref[:, pl.ds(pair, 128)]
    taken = taps[...]
    low = low_lanes(taken.shape)
    even = jnp.where(low, taken, swap(taken))
    odd = jnp.where(low, swap(taken), taken)
    taps[...] = jnp.where(lax.rem(g, 2) == 0, even, odd)

    def wide_pieces(value):
        s1 = value.astype(BF16).astype(F32)
        rest = value - s1
        s2 = rest.astype(BF16).astype(F32)
        s3 = rest - s2
        low = low_lanes(value.shape)

        def both(a, b):
            first = jnp.where(low, a, swap(b)).astype(BF16)
            return first, jnp.where(low, swap(a), b).astype(BF16)

        return both(s1, s1), both(s2, s2), both(s1, s3)

    def turned_pieces(value, target):
        for i, piece in enumerate(split2(jnp.transpose(value))):
            target[i * HD : (i + 1) * HD, 0:keys_half] = piece[0:HD]
            target[i * HD : (i + 1) * HD, keys_half : 2 * keys_half] = piece[HD : 2 * HD]

    arrive(k_copies)
    value = kp[...].reshape(keys_half, 128)
    for i, (first, second) in enumerate(wide_pieces(value)):
        ak[0:keys_half, i * 128 : (i + 1) * 128] = first
        ak[keys_half : 2 * keys_half, i * 128 : (i + 1) * 128] = second
    turned_pieces(value, kt)

    out_parts = []
    for r in range(ROWS):
        logits = dot(ak[...], bs[r])
        raised = jnp.exp(logits - jnp.max(logits, 0, keepdims=True))
        soft = raised * (1.0 / jnp.sum(raised, 0, keepdims=True))
        soft_high, soft_low = split2(soft)
        pf[r] = soft
        ph[r] = soft_high
        plo[r] = soft_low

    arrive(v_copies)
    value = vp[...].reshape(keys_half, 128)
    for i, (first, second) in enumerate(wide_pieces(value)[0:2]):
        av[0:keys_half, i * 128 : (i + 1) * 128] = first
        av[keys_half : 2 * keys_half, i * 128 : (i + 1) * 128] = second
    turned_pieces(value, vt)
    for r in range(ROWS):
        both = dot(vt[...], ph[r]) + dot(vt[...], plo[r])
        out_parts.append(both[0:HD] + both[HD : 2 * HD])
    for r in range(2):
        op[r] = jnp.transpose(jnp.concatenate([out_parts[r], out_parts[r + 2]], 0))

    arrive(h_copies, u_copies, n_copies)
    slot = {step: i for i, step in enumerate(h_steps)}
    left, right = 7, 8 + wide
    for r in range(2):
        wx[r + 1, left : left + 1] = hb[slot[0, 1], r, 7:8]
        wx[r + 1, right : right + 1] = hb[slot[0, -1], r, 0:1]
    top = jnp.where(lat > 0, 1.0, 0.0)
    bottom = jnp.where(lat < band_count - 1, 1.0, 0.0)

    def above(low_part, own):
        return jnp.where(low_lanes(own.shape), low_part * top, swap(own))

    def below(own, high_part):
        return jnp.where(low_lanes(own.shape), swap(own), high_part * bottom)

    part = COLS // 2
    for j in range(group):
        one = slice(8 + COLS * j, 8 + COLS * j + part)
        two = slice(8 + COLS * j + part, 8 + COLS * (j + 1))
        wx[0, one] = above(hu[j], wx[2, one])
        wx[0, two] = above(swap(hu[j]), wx[2, two])
        wx[3, one] = below(wx[1, one], swap(hd[j]))
        wx[3, two] = below(wx[1, two], hd[j])
    wx[0, left : left + 1] = above(swap(hb[slot[1, 1], 1, 7:8]), wx[2, left : left + 1])
    wx[0, right : right + 1] = above(swap(hb[slot[1, -1], 1, 0:1]), wx[2, right : right + 1])
    wx[3, left : left + 1] = below(wx[1, left : left + 1], swap(hb[slot[-1, 1], 0, 7:8]))
    wx[3, right : right + 1] = below(wx[1, right : right + 1], swap(hb[slot[-1, -1], 0, 0:1]))

    for r in range(2):
        value = wx[r + 1, 8 : 8 + wide]
        for a in (-1, 0, 1):
            for b in (-1, 0, 1):
                tap = 3 * (a + 1) + (b + 1)
                value = value + taps[tap : tap + 1] * wx[r + 1 - a, 8 - b : 8 - b + wide]
        high = value.astype(BF16).astype(F32)
        low = value - high
        ro[r] = both_low(high, low).astype(BF16)
        ro[r + 2] = both_high(high, low).astype(BF16)
        o1, o2 = split2(jnp.transpose(value))
        for part in range(2):
            rows = slice(part * HD, (part + 1) * HD)
            for place, piece in enumerate((o1, o2, o1, o2)):
                bd[r + 2 * part, place * HD : (place + 1) * HD] = piece[rows]

    sums = []
    for a in (-1, 0, 1):
        for b in (-1, 0, 1):
            total = jnp.sum(
                op[0] * wx[1 - a, 8 - b : 8 - b + wide]
                + op[1] * wx[2 - a, 8 - b : 8 - b + wide],
                0,
                keepdims=True,
            )
            sums.append(total + swap(total))
    first = jnp.concatenate(sums[0:8], 0)
    line = lax.broadcasted_iota(jnp.int32, (8, 128), 0)
    last = jnp.where(line == 0, jnp.broadcast_to(sums[8], (8, 128)), 0.0)
    tap_tile = jnp.where(low_lanes((8, 128)), first, last)

    tzs[...] = tap_tile
    tz_copies = phase(tzr.at[pl.ds(0, nz - 1)], tz_s, tz_r)
    for e, peer in enumerate(z_peers):
        send(tzs, tzr.at[z], tz_s, tz_r, peer)
    tzr[z] = tap_tile

    def summed(highs, lows, right):
        total = dot(highs[0], right[0]) + dot(lows[0], right[0])
        for r in range(1, ROWS):
            total = total + dot(highs[r], right[r]) + dot(lows[r], right[r])
        total = total + swap(total)
        first = total[0:keys_half]
        total = jnp.where(low_lanes(first.shape), first, total[keys_half : 2 * keys_half])
        return total.reshape(ny * group, pairs, 128)

    def spread(source, target, send_sem, recv_sem):
        copies = phase(target.at[pl.ds(0, plane)], send_sem, recv_sem)
        for e, peer in enumerate(f_peers):
            a, b = far[e]
            block = source.at[around(y, a, ny) * group + around(g, b, group)]
            send(block, target.at[here], send_sem, recv_sem, peer)
        target[here] = source[here]
        return copies

    dvb[...] = summed(ph, plo, ro)
    rv_copies = spread(dvb, dvr, rv_s, rv_r)

    query_parts = []
    for r in range(ROWS):
        soft = pf[r]
        prob_grad = dot(av[...], bd[r])
        row_dot = jnp.sum(soft * prob_grad, 0, keepdims=True)
        grad_high, grad_low = split2(soft * (prob_grad - row_dot))
        dh[r] = grad_high
        dlo[r] = grad_low
        both = dot(kt[...], grad_high) + dot(kt[...], grad_low)
        query_parts.append((both[0:HD] + both[HD : 2 * HD]) * (HD ** -0.5))

    dkb[...] = summed(dh, dlo, rq)
    rk_copies = spread(dkb, dkr, rk_s, rk_r)

    for r in range(2):
        dqs[r] = jnp.transpose(jnp.concatenate([query_parts[r], query_parts[r + 2]], 0))
    d_copies = phase(dqr.at[pl.ds(0, group - 1)], d_s, d_r)
    for e, peer in enumerate(x_peers):
        to = pl.multiple_of(around(g, e + 1, group) * COLS, 8)
        source = dqs.at[:, pl.ds(to, COLS), :]
        send(source, dqr.at[g], d_s, d_r, peer)
    dqr[g] = dqs[:, pl.ds(own_q, COLS), :]

    arrive(tz_copies)
    total = tzr[0]
    for i in range(1, nz):
        total = total + tzr[i]
    txs[...] = total
    tx_copies = phase(txr.at[pl.ds(0, plane)], tx_s, tx_r)
    for e, peer in enumerate(f_peers):
        send(txs, txr.at[here], tx_s, tx_r, peer)
    txr[here] = total

    arrive(rv_copies)
    total = dvr[0:group]
    for i in range(1, ny):
        total = total + dvr[i * group : (i + 1) * group]
    dvt[...] = total.reshape(group * pairs, 128)
    arrive(rk_copies)
    total = dkr[0:group]
    for i in range(1, ny):
        total = total + dkr[i * group : (i + 1) * group]
    dkt[...] = total.reshape(group * pairs, 128)
    for i in range(pairs):
        key_part = dkt[pl.ds(i, group, stride=pairs)]
        value_part = dvt[pl.ds(i, group, stride=pairs)]
        zs[i] = both_low(key_part, value_part)
        zs[i + pairs] = both_high(key_part, value_part)
    rz_copies = phase(rsz.at[pl.ds(0, nz - 1)], rz_s, rz_r)
    for e, peer in enumerate(z_peers):
        to = around(z, z_steps[e], nz)
        send(zs.at[to], rsz.at[z], rz_s, rz_r, peer)
    rsz[z] = zs[z]

    arrive(d_copies)
    for m in range(group // 2):
        cut = slice(m * 128, (m + 1) * 128)
        for r in range(2):
            dq_ref[r, :, cut] = both_low(dqr[2 * m, r], dqr[2 * m + 1, r])
            dq_ref[r + 2, :, cut] = both_high(dqr[2 * m, r], dqr[2 * m + 1, r])

    arrive(tx_copies)
    tiles = []
    for j in range(group):
        total = txr[j]
        for i in range(1, ny):
            total = total + txr[i * group + j]
        tiles.append(total)
    square = tiles[0] * tiles[0]
    for tile in tiles[1:]:
        square = square + tile * tile
    mean = jnp.sum(square) * (1.0 / (9 * channels))
    scale = jnp.sqrt(jnp.full((8, 128), mean, F32) + 1e-6)
    for m in range(group // 2):
        cut = slice(m * 128, (m + 1) * 128)
        one, two = tiles[2 * m], tiles[2 * m + 1]
        tu_ref[0:8, cut] = both_low(one, two) / scale
        tu_ref[8:9, cut] = (both_high(one, two) / scale)[0:1]

    arrive(rz_copies)
    total = rsz[0]
    for i in range(1, nz):
        total = total + rsz[i]
    for m in range(group // 2):
        cut = slice(m * 128, (m + 1) * 128)
        one, two = total[2 * m : 2 * m + 1], total[2 * m + 1 : 2 * m + 2]
        dk_ref[:, cut] = both_low(one, two)
        dv_ref[:, cut] = both_high(one, two)
    for copy in started:
        copy.wait_send()


def leave(*refs):
    count = len(refs) // 2
    sems = refs[-1]
    copies = []
    for i in range(count):
        copies.append(pltpu.make_async_copy(refs[i], refs[count + i], sems.at[i]))
        copies[i].start()
    for copy in copies:
        copy.wait()


def put_out(results):
    count = len(results)
    return pl.pallas_call(
        leave,
        out_shape=tuple(jax.ShapeDtypeStruct(r.shape, r.dtype) for r in results),
        in_specs=[pl.BlockSpec(memory_space=pltpu.VMEM)] * count,
        out_specs=(pl.BlockSpec(memory_space=pltpu.HBM),) * count,
        scratch_shapes=[pltpu.SemaphoreType.DMA((count,))],
    )(*[pltpu.with_memory_space_constraint(r, pltpu.VMEM) for r in results])


def body(sizes, queries, key_rows, value_rows, cotangent, conv_taps):
    nx, ny, nzl, nzh = sizes
    group = 2 * nx
    nz = nzl * nzh
    wide = group * COLS
    keys = ny * nz * group
    pairs = nz // 2
    channels = group * HD
    vmem = pltpu.VMEM
    scratch = [
        vmem((ROWS, COLS, channels), F32),
        vmem((ROWS, COLS, channels), F32),
        vmem((1, channels), F32),
        vmem((1, channels), F32),
        vmem((9, channels), F32),
        pltpu.SemaphoreType.DMA((5,)),
        vmem((group, 2, COLS, 128), F32),
        vmem((group, 2, COLS, 128), F32),
        vmem((4, wide + 16, 128), F32),
        vmem((2, wide, 128), F32),
        vmem((nz * group, 128), F32),
        vmem((group, pairs, 128), F32),
        vmem((group, pairs, 128), F32),
        vmem((ny * group, pairs, 128), F32),
        vmem((ny * group, pairs, 128), F32),
        vmem((group, COLS // 2, 128), F32),
        vmem((group, COLS // 2, 128), F32),
        vmem((group, COLS // 2, 128), F32),
        vmem((group, COLS // 2, 128), F32),
        vmem((6, 2, 8, 128), F32),
        vmem((16, 128), F32),
        vmem((ROWS, 6 * HD, wide), BF16),
        vmem((ROWS, 4 * HD, wide), BF16),
        vmem((ROWS, wide, 128), BF16),
        vmem((ROWS, wide, 128), BF16),
        vmem((keys, 6 * HD), BF16),
        vmem((keys, 4 * HD), BF16),
        vmem((128, keys), BF16),
        vmem((128, keys), BF16),
        vmem((ROWS, keys, wide), F32),
        vmem((ROWS, keys, wide), BF16),
        vmem((ROWS, keys, wide), BF16),
        vmem((ROWS, keys, wide), BF16),
        vmem((ROWS, keys, wide), BF16),
        vmem((2, wide, 128), F32),
        vmem((2, wide, 128), F32),
        vmem((group, 2, COLS, 128), F32),
        vmem((ny * group, pairs, 128), F32),
        vmem((ny * group, pairs, 128), F32),
        vmem((ny * group, pairs, 128), F32),
        vmem((ny * group, pairs, 128), F32),
        vmem((group * pairs, 128), F32),
        vmem((group * pairs, 128), F32),
        vmem((nz, group, 128), F32),
        vmem((nz, group, 128), F32),
        vmem((8, 128), F32),
        vmem((nz, 8, 128), F32),
        vmem((8, 128), F32),
        vmem((ny * group, 8, 128), F32),
    ]
    scratch += [pltpu.SemaphoreType.DMA] * 28
    scratch.append(pltpu.SemaphoreType.REGULAR)
    whole = pl.BlockSpec(memory_space=pltpu.VMEM)
    results = pl.pallas_call(
        functools.partial(kernel, sizes),
        out_shape=(
            jax.ShapeDtypeStruct((ROWS, COLS, channels), F32),
            jax.ShapeDtypeStruct((1, channels), F32),
            jax.ShapeDtypeStruct((1, channels), F32),
            jax.ShapeDtypeStruct((9, channels), F32),
        ),
        in_specs=[pl.BlockSpec(memory_space=pltpu.HBM)] * 5,
        out_specs=(whole,) * 4,
        scratch_shapes=scratch,
        compiler_params=pltpu.CompilerParams(
            collective_id=0, has_side_effects=True, vmem_limit_bytes=48 << 20
        ),
    )(*[pltpu.with_memory_space_constraint(a, pltpu.HBM) for a in (queries, cotangent, key_rows, value_rows, conv_taps)])
    return put_out(results)


def solution(mesh):
    sizes = (NX, NY, mesh.shape["lon"] // (2 * NX), mesh.shape["lat"] // NY)
    placed = (
        P("lat", "lon", None),
        P(("lat", "lon"), None),
        P(("lat", "lon"), None),
        P("lat", "lon", None),
        P(),
    )
    return jax.shard_map(
        functools.partial(body, sizes),
        mesh=mesh,
        in_specs=placed,
        out_specs=(P("lat", "lon", None), P(("lat", "lon"), None), P(("lat", "lon"), None), P()),
        check_vma=False,
    )
```
